32 devices in a mesh: blk: 16 (over z, x, core), mp: 2 (over y).
Axes of the slice: x: 2, y: 2, z: 4, core: 2. Of those that a mesh axis runs over, the one named last changes fastest.
Arguments:
- features: bfloat16 [16, 2, 2, 256, 1280], P('blk', None, None, None, 'mp'), may hold values from -62 to 62
- w_query: bfloat16 [1280, 1280], P(None, 'mp'), may hold values from -2 to 2
- w_key: bfloat16 [1280, 1280], P(None, 'mp'), may hold values from -2 to 2
- w_value: bfloat16 [1280, 1280], P(None, 'mp'), may hold values from -0.15625 to 0.15625
- w_out: bfloat16 [1280, 1280], P('mp'), may hold values from -0.15625 to 0.15625
- w_head: bfloat16 [1280, 64], replicated, may hold values from -0.15625 to 0.15625
- offsets: int32 [16], P('blk'), may hold values from 0 to 255, as said below
- blend_mask: int32 [16, 64, 64], P('blk'), may hold values from 1 to 4
Outputs:
- panorama: float32 [2, 256, 256], P(None, 'blk')
The draws below stay inside these ranges and needn't reach their ends.
Inputs may be any that keep to these rules, and one draw needn't show every extreme that they name: offsets[w] = 16 * w + s for one s shared by all windows, 0 <= s < 16.
All inputs are finite; a program needn't handle non-finite values.
Results may differ from the reference program's by a relative error of at most 0.0064.
Values may be sent and summed in bfloat16 or wider, within the bound.
No kernel may reach another device: no remote copies, remote signals or barrier semaphores. Data moves between devices by JAX's collectives and lax.ppermute only.
A program may use at most 64 MiB of HBM per device.

```python
import jax
import jax.numpy as jnp
from jax import lax

D = 1280
HEADS = 20
HEAD = 64
BATCH = 2
GRID = 16
PATCH = 4
CHAN = 4
STRIDE = 16
TOK = 256
WINDOW = 64
LAT = 256
OUTW = 64
NWIN = 16
WIDTH = 256


def draw_features(key, part):
    normal_draw = jnp.clip(jax.random.normal(jax.random.fold_in(key, 11), (NWIN, BATCH, 2, TOK, D), jnp.float32), -6.0, 6.0)
    return normal_draw.astype(jnp.bfloat16)


def head_weight(key, salt):
    normal_draw = jnp.clip(jax.random.normal(jax.random.fold_in(key, salt), (D, D), jnp.float32), -6.0, 6.0) / D ** 0.5
    normal_draw = jnp.clip(normal_draw, -2.0, 2.0)
    return normal_draw.astype(jnp.bfloat16)


def draw_w_query(key, part):
    return head_weight(key, 21)


def draw_w_key(key, part):
    return head_weight(key, 22)


def draw_offsets(key, part):
    shared = jax.random.randint(jax.random.fold_in(key, 31), (), 0, STRIDE, jnp.int32)
    return (STRIDE * jnp.arange(NWIN, dtype=jnp.int32) + shared).astype(jnp.int32)


def touch_ends(values, stream_key, low, high):
    place = [jax.random.randint(jax.random.fold_in(stream_key, axis), (), 0, length) for axis, length in enumerate(values.shape)]
    main_axis = values.shape.index(max(values.shape))
    neighbour = place[:main_axis] + [(place[main_axis] + 1) % values.shape[main_axis]] + place[main_axis + 1:]
    return values.at[tuple(place)].set(low).at[tuple(neighbour)].set(high)


def steps_of(own_key, shape, shards, low, top_value):
    factor_of, own = 1.0, jax.random.fold_in(own_key, 6)
    for axis_at, parts in shards:
        heights = jnp.exp(jax.random.uniform(jax.random.fold_in(own, axis_at), (parts,), jnp.float32, low / len(shards), top_value / len(shards)))
        factor_of = factor_of * jnp.repeat(heights, shape[axis_at] // parts).reshape([-1 if axis == axis_at else 1 for axis in range(len(shape))])
    return factor_of


def noise(own_key, shape, scale, most, split=(), held_as=jnp.bfloat16):
    result = scale * jax.random.normal(own_key, shape, jnp.float32)
    if split:
        result = result * steps_of(own_key, shape, split, -0.22, 0.18)
    return jnp.clip(result, -most, most).astype(held_as)


def setup_inputs(seed: int = 0) -> dict:
    key_of = jax.random.split(jax.random.key(seed), 9)
    return {
        "features": draw_features(jax.random.fold_in(key_of[8], 71), 0),
        "w_query": draw_w_query(jax.random.fold_in(key_of[8], 71), 0),
        "w_key": draw_w_key(jax.random.fold_in(key_of[8], 71), 0),
        "w_value": noise(key_of[3], (D, D), D ** -0.5, 0.15625, ((1, 2),)),
        "w_out": noise(key_of[4], (D, D), D ** -0.5, 0.15625, ((0, 2),)),
        "w_head": noise(key_of[5], (D, OUTW), D ** -0.5, 0.15625),
        "offsets": draw_offsets(jax.random.fold_in(key_of[8], 71), 0),
        "blend_mask": touch_ends(jax.random.randint(key_of[7], (NWIN, WINDOW, WINDOW), 1, 5), jax.random.fold_in(key_of[7], 1), 1, 4).astype(jnp.int32),
    }


guidance = 3.0

def window_eps(window_data, w_query, w_key, w_value, w_out, w_head):
    token_rows = window_data.reshape(-1, D).astype(jnp.float32)
    row_mean = lax.optimization_barrier(jnp.mean(token_rows, axis=1, keepdims=True))
    centred = token_rows - row_mean
    row_var = lax.optimization_barrier(jnp.mean(centred * centred, axis=1, keepdims=True))
    normed = (centred * lax.rsqrt(row_var + 1e-05)).astype(jnp.bfloat16)
    sequences = BATCH * 2
    queries = jnp.dot(normed, w_query, preferred_element_type=jnp.float32).astype(jnp.bfloat16).reshape(sequences, TOK, HEADS, HEAD)
    key_rows = jnp.dot(normed, w_key, preferred_element_type=jnp.float32).astype(jnp.bfloat16).reshape(sequences, TOK, HEADS, HEAD)
    value_rows = jnp.dot(normed, w_value, preferred_element_type=jnp.float32).astype(jnp.bfloat16).reshape(sequences, TOK, HEADS, HEAD)
    scores = jnp.einsum('sqhd,skhd->shqk', queries.astype(jnp.float32), key_rows.astype(jnp.float32)) / HEAD ** 0.5
    scores = scores - lax.optimization_barrier(jnp.max(scores, axis=3, keepdims=True))
    expont = jnp.exp(scores)
    attend = (expont / lax.optimization_barrier(jnp.sum(expont, axis=3, keepdims=True))).astype(jnp.bfloat16)
    context = jnp.einsum('shqk,skhd->sqhd', attend.astype(jnp.float32), value_rows.astype(jnp.float32)).astype(jnp.bfloat16).reshape(-1, D)
    attention = jnp.dot(context, w_out, preferred_element_type=jnp.float32)
    tok_out = jnp.dot(token_rows + attention, w_head.astype(jnp.float32), precision=lax.Precision.HIGHEST)
    tok_out = tok_out.reshape(BATCH, 2, TOK, OUTW)
    guided = tok_out[:, 0] + guidance * (tok_out[:, 1] - tok_out[:, 0])
    spread = guided.reshape(BATCH, GRID, GRID, PATCH, PATCH, CHAN).transpose(0, 2, 3, 1, 4, 5)
    return spread.reshape(BATCH, WINDOW, LAT)

def reference(features, w_query, w_key, w_value, w_out, w_head, offsets, blend_mask):

    def one_window(window_data):
        return window_eps(window_data, w_query, w_key, w_value, w_out, w_head)
    spread_all = lax.map(one_window, features)
    weight = blend_mask.astype(jnp.float32)
    weight_wide = jnp.repeat(weight, CHAN, axis=2)
    columns = ((offsets[:, None] + jnp.arange(WINDOW, dtype=jnp.int32)[None, :]) % WIDTH).astype(jnp.int32).reshape(-1)
    weighted = (spread_all * weight_wide[:, None]).transpose(1, 0, 2, 3).reshape(BATCH, NWIN * WINDOW, LAT)
    numerator = jnp.zeros((BATCH, WIDTH, LAT), jnp.float32).at[:, columns].add(weighted)
    weight_total = jnp.zeros((WIDTH, WINDOW), jnp.float32).at[columns].add(weight.reshape(-1, WINDOW))
    return numerator / jnp.repeat(weight_total, CHAN, axis=1)[None]
```

```python
import functools
import math

import jax
import jax.numpy as jnp
from jax import lax
from jax.experimental import pallas as pl
from jax.experimental.pallas import tpu as pltpu
from jax.sharding import PartitionSpec as P

HEAD = 64
GRID = 16
PATCH = 4
CHAN = 4
STRIDE = 16
WINDOW = 64
OUTW = 64

guidance = 3.0

F32 = jnp.float32
BF16 = jnp.bfloat16
LAT = WINDOW * CHAN
PIECES = WINDOW // STRIDE + 1
FRAME = PIECES * STRIDE
PAIR = 2 * HEAD
LANES = 128
HALVES = LAT // LANES
NT = (((1,), (1,)), ((), ()))


def dot(a, b):
    return jnp.dot(a, b, preferred_element_type=F32)


def split2(x):
    high = x.astype(BF16)
    return high, (x - high.astype(F32)).astype(BF16)


def iota(shape, axis):
    return lax.broadcasted_iota(jnp.int32, shape, axis)


def prepare(
    place,
    features,
    w_query,
    w_key,
    w_value,
    w_out,
    w_head,
    mask,
    own_acc,
    own_mean,
    own_square,
    column_sum,
    far_weights,
    out_weights,
    direct,
    spread_map,
    mask_tile,
    mask_keep,
    mask_send,
    mask_frame,
):
    half = features.shape[-1]
    width = w_query.shape[1]
    sequences = own_acc.shape[0]
    tokens = own_acc.shape[1]
    side = place[0]
    shift = place[1]
    near = pl.ds(pl.multiple_of(side * half, 128), half)
    far = pl.ds(pl.multiple_of((1 - side) * half, 128), half)
    repeat_map = (iota((WINDOW, LAT), 1) // CHAN == iota((WINDOW, LAT), 0)).astype(BF16)
    wide = dot(mask[0].astype(F32).astype(BF16), repeat_map)
    for h in range(HALVES):
        lanes = slice(h * LANES, (h + 1) * LANES)
        mask_frame[h, :WINDOW] = wide[:, lanes]
        mask_frame[h, WINDOW:] = jnp.zeros((FRAME - WINDOW, LANES), F32)
        for a in range(PATCH):
            places = slice(a * LAT + h * LANES, a * LAT + (h + 1) * LANES)
            mask_tile[:, places] = mask_frame[h, pl.ds(a, GRID, stride=PATCH), :]
        rolled = pltpu.roll(mask_frame[h], shift, 0)
        for t in range(PIECES):
            piece = rolled[t * STRIDE : (t + 1) * STRIDE]
            (mask_send if t % 2 else mask_keep)[t // 2, :, lanes] = piece
    part = OUTW // PATCH
    rows, columns = iota((2 * OUTW, PATCH * LAT), 0) % OUTW, iota((2 * OUTW, PATCH * LAT), 1)
    spread_map[...] = (
        (rows // part == columns // LAT) & (rows % part == columns % part)
    ).astype(BF16)
    ones = jnp.ones((8, w_query.shape[0]), BF16)
    for j, w in enumerate((w_query, w_key, w_value)):
        column_sum[:, j * width : (j + 1) * width] = dot(ones, w[...])
        far_weights[:, j * width : (j + 1) * width] = w[far, :]
    high, low = split2(dot(w_out[...], w_head[...]))
    out_weights[:half] = high
    out_weights[half:] = low
    for s in range(sequences):
        x = features[0, s // 2, s % 2]
        xf = x.astype(F32)
        mean = jnp.mean(xf, axis=1, keepdims=True)
        centred = xf - mean
        own_mean[s] = mean
        own_square[s] = jnp.sum(centred * centred, axis=1, keepdims=True)
        direct[s] = dot(x, w_head[near, :])
        for j, w in enumerate((w_query, w_key, w_value)):
            own_acc[s, :, j * width : (j + 1) * width] = dot(x, w[near, :])


def attend(
    s,
    last,
    place,
    arrived,
    own_acc,
    own_mean,
    own_square,
    column_sum,
    far_weights,
    out_weights,
    direct,
    *rest,
):
    if s % 2 == 0:
        guided_out, q_even, q_odd, keys, values, context = rest
    else:
        spread_map, mask_tile, guided_in = rest[:3]
        rest = rest[3:]
        if last:
            before = rest[: 2 * (s // 2)]
            rest = rest[2 * (s // 2) :]
        keep, send, frame, q_even, q_odd, keys, values, context = rest
    half = arrived.shape[-1]
    width = far_weights.shape[1] // 3
    tokens = arrived.shape[-2]
    x = arrived[...]
    xf = x.astype(F32)
    far_mean = jnp.mean(xf, axis=1, keepdims=True)
    centred = xf - far_mean
    far_square = jnp.sum(centred * centred, axis=1, keepdims=True)
    near_mean = own_mean[s]
    gap = near_mean - far_mean
    mean = 0.5 * (near_mean + far_mean)
    var = (own_square[s] + far_square + gap * gap * (0.5 * half)) / (2.0 * half)
    scale = lax.rsqrt(var + 1e-05)
    offset = mean * scale

    def project(j):
        columns = slice(j * width, (j + 1) * width)
        total = own_acc[s, :, columns] + dot(x, far_weights[:, columns])
        return total, column_sum[0:1, columns]

    factor = math.log2(math.e) / HEAD**0.5
    total, sums = project(0)
    queries = total * (scale * factor) - (offset * factor) * sums
    even = iota((1, width), 1) % PAIR < HEAD
    q_even[...] = jnp.where(even, queries, 0.0).astype(BF16)
    q_odd[...] = jnp.where(even, 0.0, queries).astype(BF16)
    total, sums = project(1)
    keys[...] = (total * scale - offset * sums).astype(BF16)
    total, sums = project(2)
    values[...] = (total * scale - offset * sums).astype(BF16)
    first = iota((1, PAIR), 1) < HEAD
    ones = jnp.ones((tokens, PAIR), BF16)
    none = jnp.zeros((tokens, PAIR), BF16)
    ones_even = jnp.where(first, ones, none)
    ones_odd = jnp.where(first, none, ones)
    for p in range(width // PAIR):
        columns = slice(p * PAIR, (p + 1) * PAIR)
        k = keys[:, columns]
        v = values[:, columns]
        probs = []
        for q in (q_even, q_odd):
            scores = lax.dot_general(q[:, columns], k, NT, preferred_element_type=F32)
            top = jnp.max(scores, axis=1, keepdims=True)
            probs.append(jnp.exp2(scores - top).astype(BF16))
        stacked = jnp.concatenate(
            [
                jnp.concatenate([jnp.where(first, v, none), ones_even], axis=1),
                jnp.concatenate([jnp.where(first, none, v), ones_odd], axis=1),
            ],
            axis=0,
        )
        both = dot(jnp.concatenate(probs, axis=1), stacked)
        context[:, columns] = (both[:, :PAIR] / both[:, PAIR:]).astype(BF16)
    ctx = context[...]
    out = dot(ctx, out_weights[:width]) + dot(ctx, out_weights[width:]) + direct[s]
    if s % 2 == 0:
        guided_out[...] = (1.0 - guidance) * out
        return
    guided = guidance * out + guided_in[...]
    tiled = dot(jnp.concatenate(split2(guided), axis=1), spread_map[...])
    lane_row = iota((1, PATCH * LAT), 1) % LAT // (LAT // GRID)
    spread = tiled[:GRID]
    for r in range(1, GRID):
        spread = jnp.where(lane_row == r, tiled[r * GRID : (r + 1) * GRID], spread)
    spread = spread * mask_tile[...]
    shift = place[1]
    slot = s // 2 if last else 0
    if last:
        for b in range(slot):
            keep[b] = before[2 * b][0]
            send[b] = before[2 * b + 1][0]
    for h in range(HALVES):
        lanes = slice(h * LANES, (h + 1) * LANES)
        for a in range(PATCH):
            places = slice(a * LAT + h * LANES, a * LAT + (h + 1) * LANES)
            frame[h, pl.ds(a, GRID, stride=PATCH), :] = spread[:, places]
        frame[h, WINDOW:] = jnp.zeros((FRAME - WINDOW, LANES), F32)
        rolled = pltpu.roll(frame[h], shift, 0)
        for t in range(PIECES):
            piece = rolled[t * STRIDE : (t + 1) * STRIDE]
            (send if t % 2 else keep)[slot, t // 2, :, lanes] = piece


def in_vmem(shape, dtype):
    return pltpu.VMEM(shape, dtype)


def call(kernel, name, args, outs, scratch, flops, limit):
    specs = [pl.BlockSpec(memory_space=pltpu.SMEM)]
    specs += [pl.BlockSpec(memory_space=pltpu.VMEM)] * (len(args) - 1)
    return pl.pallas_call(
        kernel,
        out_shape=[in_vmem(shape, dtype) for shape, dtype in outs],
        in_specs=specs,
        out_specs=[pl.BlockSpec(memory_space=pltpu.VMEM)] * len(outs),
        scratch_shapes=scratch,
        compiler_params=pltpu.CompilerParams(vmem_limit_bytes=limit),
        cost_estimate=pl.CostEstimate(flops=flops, bytes_accessed=4 << 20, transcendentals=0),
        name=name,
    )(*args)


def blend(keep, send, parity, count):
    def moved(x, by):
        return lax.ppermute(x, "blk", [(i, (i + by) % count) for i in range(count)])

    got = lax.ppermute(send, "blk", [(i, i ^ 1) for i in range(count)])
    odd = parity == 1
    zero = jnp.zeros_like(got[:, 0])
    near = keep[:, 0] + jnp.where(odd, got[:, 0], zero)
    next_chip = keep[:, 1] + jnp.where(odd, got[:, 1], got[:, 0])
    second_chip = keep[:, 2] + jnp.where(odd, zero, got[:, 1])
    next_chip = moved(next_chip, 2)
    second_chip = moved(second_chip, 4)
    return near + next_chip + second_chip


def shards(features, w_query, w_key, w_value, w_out, w_head, offsets, blend_mask):
    batch_count, passes, tokens, half = features.shape[1:]
    width = w_query.shape[1]
    sequences = batch_count * passes
    count = lax.axis_size("blk")
    block = lax.axis_index("blk")
    side = lax.axis_index("mp")
    swap = [(0, 1), (1, 0)]
    arrived = [
        lax.ppermute(features[0, s // 2, s % 2], "mp", swap) for s in range(sequences)
    ]
    shift = offsets[0] - STRIDE * block
    place = jnp.stack([side, shift]).astype(jnp.int32)
    keeps = PIECES // 2 + 1
    sends = PIECES // 2
    outs = [
        ((sequences, tokens, 3 * width), F32),
        ((sequences, tokens, 1), F32),
        ((sequences, tokens, 1), F32),
        ((8, 3 * width), F32),
        ((half, 3 * width), BF16),
        ((2 * half, OUTW), BF16),
        ((sequences, tokens, OUTW), F32),
        ((2 * OUTW, PATCH * LAT), BF16),
        ((GRID, PATCH * LAT), F32),
        ((keeps, STRIDE, LAT), F32),
        ((sends, STRIDE, LAT), F32),
    ]
    *shared, spread_map, mask_tile, mask_keep, mask_send = call(
        prepare,
        "prepare",
        (place, features, w_query, w_key, w_value, w_out, w_head, blend_mask),
        outs,
        [pltpu.VMEM((HALVES, FRAME, LANES), F32)],
        2 * sequences * tokens * half * 3 * width,
        48 << 20,
    )
    parity = block % 2
    weight_total = blend(mask_keep[None], mask_send[None], parity, count)
    work = [pltpu.VMEM((tokens, width), BF16)] * 5
    flops = 2 * tokens * (half * 3 * width + 2 * tokens * width)
    pieces = []
    for b in range(batch_count):
        last = b == batch_count - 1
        (guided,) = call(
            functools.partial(attend, 2 * b, False),
            f"attend_{b}_0",
            (place, arrived[2 * b], *shared),
            [((tokens, OUTW), F32)],
            work,
            flops,
            24 << 20,
        )
        planes = b + 1 if last else 1
        pieces += call(
            functools.partial(attend, 2 * b + 1, last),
            f"attend_{b}_1",
            (place, arrived[2 * b + 1], *shared, spread_map, mask_tile, guided)
            + (tuple(pieces) if last else ()),
            [
                ((planes, keeps, STRIDE, LAT), F32),
                ((planes, sends, STRIDE, LAT), F32),
            ],
            [pltpu.VMEM((HALVES, FRAME, LANES), F32)] + work,
            flops,
            24 << 20,
        )
    part = blend(pieces[-2], pieces[-1], parity, count)
    total = part + lax.ppermute(part, "mp", swap)
    return total / weight_total


def solution(mesh):
    return jax.shard_map(
        shards,
        mesh=mesh,
        in_specs=(
            P("blk", None, None, None, "mp"),
            P(None, "mp"),
            P(None, "mp"),
            P(None, "mp"),
            P("mp", None),
            P(),
            P("blk"),
            P("blk", None, None),
        ),
        out_specs=P(None, "blk", None),
        check_vma=False,
    )
```

```python
import functools
import math

import jax
import jax.numpy as jnp
from jax import lax
from jax.experimental import pallas as pl
from jax.experimental.pallas import tpu as pltpu
from jax.sharding import PartitionSpec as P


HEAD = 64
GRID = 16
PATCH = 4
CHAN = 4
STRIDE = 16
WINDOW = 64
OUTW = 64

guidance = 3.0


F32 = jnp.float32
BF16 = jnp.bfloat16
LAT = WINDOW * CHAN
LANES = 128
HALVES = LAT // LANES
BLOCK = 2 * STRIDE
BLOCKS = -(-(WINDOW + BLOCK - 1) // BLOCK)
FRAME = BLOCKS * BLOCK
PACKED = BLOCK * WINDOW // LAT
PAIR = 2 * HEAD
TRIPLE = 3 * PAIR
TAIL = 128
LAST_COLUMNS = 256


def dot(a, b):
    return jnp.dot(a, b, preferred_element_type=F32)


def dot_nt(a, b):
    return lax.dot_general(a, b, (((1,), (1,)), ((), ())), preferred_element_type=F32)


def moments(x):
    mean = jnp.mean(x, axis=1, keepdims=True)
    centred = x - mean
    return mean, jnp.sum(centred * centred, axis=1, keepdims=True)


def merged(a, b, a_count, b_count):
    count = a_count + b_count
    gap = b[0] - a[0]
    mean = a[0] + gap * (b_count / count)
    return mean, a[1] + b[1] + gap * gap * (a_count * b_count / count)


def split2(x):
    high = x.astype(BF16)
    return high, (x - high.astype(F32)).astype(BF16)


def iota(shape, axis):
    return lax.broadcasted_iota(jnp.int32, shape, axis)


def repeat_map():
    return (iota((WINDOW, LAT), 1) // CHAN == iota((WINDOW, LAT), 0)).astype(BF16)


def column_groups(columns):
    pairs = columns // TRIPLE
    starts = [2 * TRIPLE * g for g in range(-(-pairs // 2))]
    return list(zip(starts, starts[1:] + [columns]))


def to_frame(frame, shift):
    frame[WINDOW:] = jnp.zeros((FRAME - WINDOW, LANES), F32)
    by = shift + STRIDE * (lax.axis_index("blk") % 2)
    return pltpu.roll(frame[...], by, 0)


def window_shift(offsets):
    return offsets[0] - STRIDE * lax.axis_index("blk")


def prepare(
    offsets,
    features,
    w_query,
    w_key,
    w_value,
    w_out,
    w_head,
    mask,
    own_acc,
    own_mean,
    own_square,
    own_tail,
    near_sum,
    far_weights,
    out_weights,
    spread_map,
    mask_tile,
    mask_blocks,
    frame,
    held,
    near_weights,
    out_rows,
    sem,
):
    half = features.shape[-1]
    width = w_query.shape[1]
    sequences, _, columns = own_acc.shape
    passes = features.shape[2]
    pairs = width // PAIR
    side = lax.axis_index("mp")
    near = pl.ds(pl.multiple_of(side * half, LANES), half)
    far = pl.ds(pl.multiple_of((1 - side) * half, LANES), half)
    loads = [(features.at[0], held)]
    for p in range(pairs):
        for j, w in enumerate((w_query, w_key, w_value)):
            source = pl.ds(p * PAIR, PAIR)
            place = pl.ds(p * TRIPLE + j * PAIR, PAIR)
            loads.append((w.at[near, source], near_weights.at[:, place]))
    loads.append((w_out, out_rows))
    for p in range(pairs):
        for j, w in enumerate((w_query, w_key, w_value)):
            source = pl.ds(p * PAIR, PAIR)
            place = pl.ds(p * TRIPLE + j * PAIR, PAIR)
            loads.append((w.at[far, source], far_weights.at[pl.ds(TAIL, half), place]))
    loads = [pltpu.make_async_copy(a, b, sem.at[i]) for i, (a, b) in enumerate(loads)]
    for load in loads:
        load.start()
    shift = window_shift(offsets)
    plain = mask[0].astype(F32)
    wide = dot(plain.astype(BF16), repeat_map())
    for h in range(HALVES):
        lanes = slice(h * LANES, (h + 1) * LANES)
        frame[:WINDOW] = wide[:, lanes]
        for a in range(PATCH):
            places = slice(a * LAT + h * LANES, a * LAT + (h + 1) * LANES)
            mask_tile[:, places] = frame[pl.ds(a, GRID, stride=PATCH), :]
    frame[:WINDOW, :WINDOW] = 0.5 * plain
    frame[:WINDOW, WINDOW:] = jnp.zeros((WINDOW, LANES - WINDOW), F32)
    rolled = to_frame(frame, shift)
    for t in range(BLOCKS):
        for k in range(LAT // WINDOW):
            rows = slice(t * BLOCK + k * PACKED, t * BLOCK + (k + 1) * PACKED)
            mask_blocks[t, :, k * WINDOW : (k + 1) * WINDOW] = rolled[rows, :WINDOW]
    part = OUTW // PATCH
    rows, places = iota(spread_map.shape, 0) % OUTW, iota(spread_map.shape, 1)
    spread_map[...] = ((rows // part == places // LAT) & (rows % part == places % part)).astype(BF16)
    near_weights[:, 3 * width : 3 * width + OUTW] = w_head[:, near].T
    near_weights[:, 3 * width + OUTW :] = jnp.zeros((half, columns - 3 * width - OUTW), BF16)
    far_weights[TAIL:, 3 * width :] = jnp.zeros((half, columns - 3 * width), BF16)
    loads[0].wait()
    main = half - TAIL
    ones = jnp.ones((8, main), BF16)
    for s in range(sequences):
        x = held[s // passes, s % passes]
        own_mean[s], own_square[s] = moments(x.astype(F32))
        own_tail[s] = x[:, main:]
    done = 1
    for first, last in column_groups(columns):
        count = 3 * ((min(last, 3 * width) - first) // TRIPLE)
        for load in loads[done : done + count]:
            load.wait()
        done += count
        w = near_weights[:main, first:last]
        for s in range(sequences):
            own_acc[s, :, first:last] = dot(held[s // passes, s % passes, :, :main], w)
        near_sum[:, first:last] = dot(ones, w)
    far_weights[:TAIL] = near_weights[main:]
    loads[done].wait()
    high, low = split2(dot_nt(out_rows[...], w_head[...]))
    out_weights[:, :OUTW] = high
    out_weights[:, OUTW:] = low
    for load in loads[done + 1 :]:
        load.wait()


def cut(windows, features, *refs):
    outs, sem = refs[:-1], refs[-1]
    passes = features.shape[2]
    loads = [
        pltpu.make_async_copy(
            features.at[0, s // passes, s % passes, :, pl.ds(start, stop - start)],
            out,
            sem.at[i],
        )
        for i, ((s, start, stop), out) in enumerate(zip(windows, outs))
    ]
    for load in loads:
        load.start()
    for load in loads:
        load.wait()


def halves(x):
    odd = lax.axis_index("blk") % 2 == 1
    own, other = [], []
    for b in range(x.shape[0] // BLOCK):
        low = x[b * BLOCK : b * BLOCK + STRIDE]
        high = x[b * BLOCK + STRIDE : (b + 1) * BLOCK]
        own.append(jnp.where(odd, high, low))
        other.append(jnp.where(odd, low, high))
    weights = x[-PACKED:]
    return jnp.concatenate(own + [weights], axis=0), jnp.concatenate(other + [weights], axis=0)


def sum_chip(own, got, here, next_chip, second_chip):
    here[...] = halves(own[0] + got[0])[0]
    next_chip[...] = own[1] + got[1]
    second_chip[...] = own[2] + got[2]


def sum_far(here, across, first, second, mine, other):
    kept, passed = halves(first[...] + second[...])
    mine[...] = here[...] + across[...] + kept
    other[...] = passed


def finish(mine, got, out):
    odd = lax.axis_index("blk") % 2 == 1
    total = mine[...] + got[...]
    packed = total[-PACKED:]
    packed = jnp.where(odd, packed[:, LAT // 2 :], packed[:, : LAT // 2])
    weights = [packed[:, k * WINDOW : (k + 1) * WINDOW] for k in range(STRIDE // PACKED)]
    weights = dot(jnp.concatenate(weights, axis=0).astype(BF16), repeat_map())
    for b in range(out.shape[0]):
        out[b] = total[b * STRIDE : (b + 1) * STRIDE] / weights


def extend(
    s,
    arrived,
    own_acc,
    own_mean,
    own_square,
    own_tail,
    far_weights,
    token,
    acc,
    mean,
    square,
):
    del token
    x = arrived[...]
    near = own_mean[s], own_square[s]
    half = far_weights.shape[0] - TAIL
    mean[0], square[0] = merged(near, moments(x.astype(F32)), half, x.shape[1])
    x = jnp.concatenate([own_tail[s], x], axis=1)
    for first, last in column_groups(own_acc.shape[2]):
        w = far_weights[: x.shape[1], first:last]
        acc[0, :, first:last] = own_acc[s, :, first:last] + dot(x, w)


def attend(
    s,
    near_count,
    width,
    offsets,
    arrived,
    own_acc,
    own_mean,
    own_square,
    own_tail,
    sums_in,
    far_weights,
    out_weights,
    *rest,
):
    first_pass = s % 2 == 0
    if first_pass:
        _, guided_out = rest[:2]
        sums_out = rest[2:]
    else:
        spread_map, mask_tile, guided_in = rest[:3]
        before = rest[3:-2]
        blocks, frame = rest[-2:]
    tokens, far_count = arrived.shape
    columns = own_acc.shape[2]
    half = far_weights.shape[0] - TAIL
    slab = s if own_acc.shape[0] > 1 else 0
    x = arrived[...]
    near = own_mean[slab], own_square[slab]
    mean, square = merged(near, moments(x.astype(F32)), near_count, far_count)
    scale = lax.rsqrt(square / (near_count + far_count) + 1e-05)
    offset = mean * scale
    if near_count == half:
        x = jnp.concatenate([own_tail[s], x], axis=1)
    rows = slice(TAIL + half - x.shape[1], TAIL + half)
    start = s == 0
    if start:
        x = jnp.concatenate([x, jnp.ones((16, x.shape[1]), BF16)], axis=0)
    factor = math.log2(math.e) / HEAD**0.5
    query_scale, query_offset = scale * factor, offset * factor
    first_head = iota((1, PAIR), 1) < HEAD
    ones = jnp.ones((tokens, PAIR), BF16)
    none = jnp.zeros((tokens, PAIR), BF16)
    ones_even = jnp.where(first_head, ones, none)
    ones_odd = jnp.where(first_head, none, ones)
    out = None
    for first, last in column_groups(columns):
        total = dot(x, far_weights[rows, first:last])
        sums = sums_in[0:8, first:last]
        if start:
            sums = sums + total[tokens : tokens + 8]
            sums_out[0][:, first:last] = sums
            total = total[:tokens]
        total = total + own_acc[slab, :, first:last]
        sums = sums[0:1]
        contexts = []
        for p in range((min(last, 3 * width) - first) // TRIPLE):

            def part(j, by, less):
                places = slice(p * TRIPLE + j * PAIR, p * TRIPLE + (j + 1) * PAIR)
                return total[:, places] * by - less * sums[:, places]

            query = part(0, query_scale, query_offset)
            k = part(1, scale, offset).astype(BF16)
            v = part(2, scale, offset).astype(BF16)
            probs = []
            for q in (jnp.where(first_head, query, 0.0), jnp.where(first_head, 0.0, query)):
                scores = dot_nt(q.astype(BF16), k)
                top = jnp.max(scores, axis=1, keepdims=True)
                probs.append(jnp.exp2(scores - top).astype(BF16))
            stacked = jnp.concatenate(
                [
                    jnp.concatenate([jnp.where(first_head, v, none), ones_even], axis=1),
                    jnp.concatenate([jnp.where(first_head, none, v), ones_odd], axis=1),
                ],
                axis=0,
            )
            both = dot(jnp.concatenate(probs, axis=1), stacked)
            contexts.append((both[:, :PAIR] / both[:, PAIR:]).astype(BF16))
        here = slice(first // 3, first // 3 + len(contexts) * PAIR)
        more = dot(jnp.concatenate(contexts, axis=1), out_weights[here])
        out = more if out is None else out + more
        if last > 3 * width:
            out = out + total[:, 3 * width - first :]
    if first_pass:
        guided_out[...] = (1.0 - guidance) * out
        return
    guided = guidance * out + guided_in[...]
    tiled = dot(jnp.concatenate(split2(guided), axis=1), spread_map[...])
    lane_row = iota((1, PATCH * LAT), 1) % LAT // (LAT // GRID)
    spread = tiled[:GRID]
    for r in range(1, GRID):
        spread = jnp.where(lane_row == r, tiled[r * GRID : (r + 1) * GRID], spread)
    spread = spread * mask_tile[...]
    shift = window_shift(offsets)
    for h in range(HALVES):
        lanes = slice(h * LANES, (h + 1) * LANES)
        for a in range(PATCH):
            places = slice(a * LAT + h * LANES, a * LAT + (h + 1) * LANES)
            frame[pl.ds(a, GRID, stride=PATCH), :] = spread[:, places]
        rolled = to_frame(frame, shift)
        at = sum(x.shape[1] for x in before[:-1])
        for t in range(BLOCKS):
            blocks[t, at : at + BLOCK, lanes] = rolled[t * BLOCK : (t + 1) * BLOCK]
    at = 0
    for i, x in enumerate(before):
        if i == len(before) - 1:
            at += BLOCK
        blocks[:, at : at + x.shape[1]] = x[...]
        at += x.shape[1]


def call(kernel, args, outs, scratch=(), flops=0, limit=1 << 20, smem=0):
    specs, values = [], []
    for i, x in enumerate(args):
        space = pltpu.SMEM if i < smem else pltpu.VMEM
        if isinstance(x, tuple):
            x, space = x
            x = pltpu.with_memory_space_constraint(x, space)
        specs.append(pl.BlockSpec(memory_space=space))
        values.append(x)
    return pl.pallas_call(
        kernel,
        out_shape=[pltpu.VMEM(shape, dtype) for shape, dtype in outs],
        in_specs=specs,
        out_specs=[pl.BlockSpec(memory_space=pltpu.VMEM)] * len(outs),
        scratch_shapes=list(scratch),
        compiler_params=pltpu.CompilerParams(vmem_limit_bytes=limit),
        cost_estimate=pl.CostEstimate(flops=flops, bytes_accessed=1 << 20, transcendentals=0),
    )(*values)


def partner(x):
    count = lax.axis_size("blk")
    return lax.ppermute(x, "blk", [(i, i ^ 1) for i in range(count)])


def across(x):
    return lax.ppermute(x, "mp", [(0, 1), (1, 0)])


def moved(x, by):
    count, sides = lax.axis_size("blk"), lax.axis_size("mp")
    pairs = [
        (i * sides + m, (i + 2 * by) % count * sides + (m ^ (i % 2)))
        for i in range(count)
        for m in range(sides)
    ]
    return lax.ppermute(x, ("blk", "mp"), pairs)


def blend(blocks, batch_count):
    whole, part = blocks.shape[1:], (batch_count * STRIDE + PACKED, LAT)
    got = partner(blocks)
    here, first, second = call(sum_chip, (blocks, got), [(part, F32), (whole, F32), (whole, F32)])
    first = moved(first, 1)
    second = moved(second, 2)
    other_side = across(here)
    mine, other = call(sum_far, (here, other_side, first, second), [(part, F32)] * 2)
    return pl.pallas_call(
        finish,
        out_shape=jax.ShapeDtypeStruct((batch_count, STRIDE, LAT), F32),
        compiler_params=pltpu.CompilerParams(vmem_limit_bytes=1 << 20),
        name="finish",
    )(mine, partner(other))


def shards(features, w_query, w_key, w_value, w_out, w_head, offsets, blend_mask):
    batch_count, passes, tokens, half = features.shape[1:]
    width = w_query.shape[1]
    sequences = batch_count * passes
    columns = 3 * width + 2 * OUTW
    windows = [(s, 0, half) for s in range(sequences - 1)]
    split = max(half - LAST_COLUMNS, 0)
    if split:
        windows.append((sequences - 1, 0, split))
    windows.append((sequences - 1, split, half))
    arrived = []
    for group in (windows[:1], windows[1:]):
        parts = call(
            functools.partial(cut, group),
            ((features, pltpu.HBM),),
            [((tokens, stop - start), features.dtype) for _, start, stop in group],
            [pltpu.SemaphoreType.DMA((len(group),))],
        )
        for part in parts:
            arrived.append(across(part))
    outs = [
        ((sequences, tokens, columns), F32),
        ((sequences, tokens, 1), F32),
        ((sequences, tokens, 1), F32),
        ((sequences, tokens, TAIL), BF16),
        ((8, columns), F32),
        ((TAIL + half, columns), BF16),
        ((width, 2 * OUTW), BF16),
        ((4 * OUTW, PATCH * LAT), BF16),
        ((GRID, PATCH * LAT), F32),
        ((BLOCKS, PACKED, LAT), F32),
    ]
    weights = [(w, pltpu.HBM) for w in (w_query, w_key, w_value, w_out)]
    frame = [pltpu.VMEM((FRAME, LANES), F32)]
    prepared = call(
        prepare,
        (offsets, (features, pltpu.HBM), *weights, w_head.T, blend_mask),
        outs,
        frame
        + [
            pltpu.VMEM(features.shape[1:], features.dtype),
            pltpu.VMEM((half, columns), BF16),
            pltpu.VMEM(w_out.shape, BF16),
            pltpu.SemaphoreType.DMA((2 + 6 * (width // PAIR),)),
        ],
        2 * sequences * tokens * half * 3 * width,
        24 << 20,
        1,
    )
    acc, mean, square, tail, sums, far_weights, out_weights = prepared[:7]
    spread_map, mask_tile, mask_blocks = prepared[7:]
    own = (acc, mean, square)
    flops = 2 * tokens * (half * 3 * width + 2 * tokens * width)
    blocks = []
    token = mask_blocks
    at = 0
    for s in range(sequences):
        near, near_count = own, half
        if arrived[at].shape[1] < half:
            near = tuple(
                call(
                    functools.partial(extend, s),
                    (arrived[at], *own, tail, far_weights, (token, pl.ANY)),
                    [((1, tokens, columns), F32), ((1, tokens, 1), F32), ((1, tokens, 1), F32)],
                    (),
                    2 * tokens * arrived[at].shape[1] * 3 * width,
                    8 << 20,
                )
            )
            near_count = half + arrived[at].shape[1]
            at += 1
        args = (offsets, arrived[at], *near, tail, sums, far_weights, out_weights)
        at += 1
        scratch = ()
        if s % passes == 0:
            args += ((token, pl.ANY),)
            results = [((tokens, 2 * OUTW), F32)]
            if s == 0:
                results.append(((8, columns), F32))
        else:
            args += (spread_map, mask_tile, token)
            rows = BLOCK
            if s == sequences - 1:
                args += (*blocks, mask_blocks)
                rows = batch_count * BLOCK + PACKED
            results = [((BLOCKS, rows, LAT), F32)]
            scratch = frame
        token, *more = call(
            functools.partial(attend, s, near_count, width),
            args,
            results,
            scratch,
            flops,
            16 << 20,
            1,
        )
        if more:
            (sums,) = more
        if s % passes:
            blocks.append(token)
    return blend(blocks[-1], batch_count)


def solution(mesh):
    return jax.shard_map(
        shards,
        mesh=mesh,
        in_specs=(
            P("blk", None, None, None, "mp"),
            P(None, "mp"),
            P(None, "mp"),
            P(None, "mp"),
            P("mp", None),
            P(),
            P("blk"),
            P("blk", None, None),
        ),
        out_specs=P(None, "blk", None),
        check_vma=False,
    )
```

```python
import functools
import math

import jax
import jax.numpy as jnp
from jax import lax
from jax.experimental import pallas as pl
from jax.experimental.pallas import tpu as pltpu
from jax.sharding import PartitionSpec as P


HEAD = 64
GRID = 16
PATCH = 4
CHAN = 4
STRIDE = 16
WINDOW = 64
OUTW = 64

guidance = 3.0


F32 = jnp.float32
BF16 = jnp.bfloat16
LAT = WINDOW * CHAN
LANES = 128
HALVES = LAT // LANES
BLOCK = 2 * STRIDE
BLOCKS = -(-(WINDOW + BLOCK - 1) // BLOCK)
FRAME = BLOCKS * BLOCK
PACKED = BLOCK * WINDOW // LAT
PAIR = 2 * HEAD
TRIPLE = 3 * PAIR
TAIL = 128
LAST_COLUMNS = 256


def dot(a, b):
    return jnp.dot(a, b, preferred_element_type=F32)


def dot_nt(a, b):
    return lax.dot_general(a, b, (((1,), (1,)), ((), ())), preferred_element_type=F32)


def moments(x):
    mean = jnp.mean(x, axis=1, keepdims=True)
    centred = x - mean
    return mean, jnp.sum(centred * centred, axis=1, keepdims=True)


def merged(near, near_count, x):
    mean, square = near
    count = near_count + x.shape[1]
    gap = x - mean
    total = jnp.sum(gap, axis=1, keepdims=True)
    square = square + jnp.sum(gap * gap, axis=1, keepdims=True)
    return mean + total * (1.0 / count), square - total * total * (1.0 / count)


def split2(x):
    high = x.astype(BF16)
    return high, (x - high.astype(F32)).astype(BF16)


def iota(shape, axis):
    return lax.broadcasted_iota(jnp.int32, shape, axis)


def repeat_map():
    return (iota((WINDOW, LAT), 1) // CHAN == iota((WINDOW, LAT), 0)).astype(BF16)


def column_groups(columns):
    pairs = columns // TRIPLE
    starts = [2 * TRIPLE * g for g in range(-(-pairs // 2))]
    return list(zip(starts, starts[1:] + [columns]))


def to_frame(frame, shift):
    frame[WINDOW:] = jnp.zeros((FRAME - WINDOW, LANES), F32)
    by = shift + STRIDE * (lax.axis_index("blk") % 2)
    return pltpu.roll(frame[...], by, 0)


def window_shift(offsets):
    return offsets[0] - STRIDE * lax.axis_index("blk")


def prepare(
    offsets,
    features,
    w_query,
    w_key,
    w_value,
    w_out,
    w_head,
    mask,
    own_acc,
    own_mean,
    own_square,
    own_tail,
    near_sum,
    far_weights,
    out_weights,
    spread_map,
    mask_tile,
    mask_blocks,
    frame,
    held,
    near_weights,
    out_rows,
    sem,
):
    half = features.shape[-1]
    width = w_query.shape[1]
    sequences, _, columns = own_acc.shape
    passes = features.shape[2]
    pairs = width // PAIR
    side = lax.axis_index("mp")
    near = pl.ds(pl.multiple_of(side * half, LANES), half)
    far = pl.ds(pl.multiple_of((1 - side) * half, LANES), half)
    loads = [(features.at[0], held)]
    for p in range(pairs):
        for j, w in enumerate((w_query, w_key, w_value)):
            source = pl.ds(p * PAIR, PAIR)
            place = pl.ds(p * TRIPLE + j * PAIR, PAIR)
            loads.append((w.at[near, source], near_weights.at[:, place]))
    loads.append((w_out, out_rows))
    for p in range(pairs):
        for j, w in enumerate((w_query, w_key, w_value)):
            source = pl.ds(p * PAIR, PAIR)
            place = pl.ds(p * TRIPLE + j * PAIR, PAIR)
            loads.append((w.at[far, source], far_weights.at[pl.ds(TAIL, half), place]))
    loads = [pltpu.make_async_copy(a, b, sem.at[i]) for i, (a, b) in enumerate(loads)]
    for load in loads:
        load.start()
    shift = window_shift(offsets)
    plain = mask[0].astype(F32)
    wide = dot(plain.astype(BF16), repeat_map())
    for h in range(HALVES):
        lanes = slice(h * LANES, (h + 1) * LANES)
        frame[:WINDOW] = wide[:, lanes]
        for a in range(PATCH):
            places = slice(a * LAT + h * LANES, a * LAT + (h + 1) * LANES)
            mask_tile[:, places] = frame[pl.ds(a, GRID, stride=PATCH), :]
    frame[:WINDOW, :WINDOW] = 0.5 * plain
    frame[:WINDOW, WINDOW:] = jnp.zeros((WINDOW, LANES - WINDOW), F32)
    rolled = to_frame(frame, shift)
    for t in range(BLOCKS):
        for k in range(LAT // WINDOW):
            rows = slice(t * BLOCK + k * PACKED, t * BLOCK + (k + 1) * PACKED)
            mask_blocks[t, :, k * WINDOW : (k + 1) * WINDOW] = rolled[rows, :WINDOW]
    part = OUTW // PATCH
    rows, places = iota(spread_map.shape, 0) % OUTW, iota(spread_map.shape, 1)
    spread_map[...] = ((rows // part == places // LAT) & (rows % part == places % part)).astype(BF16)
    near_weights[:, 3 * width : 3 * width + OUTW] = w_head[:, near].T
    near_weights[:, 3 * width + OUTW :] = jnp.zeros((half, columns - 3 * width - OUTW), BF16)
    far_weights[TAIL:, 3 * width :] = jnp.zeros((half, columns - 3 * width), BF16)
    loads[0].wait()
    main = half - TAIL
    ones = jnp.ones((8, main), BF16)
    for s in range(sequences):
        x = held[s // passes, s % passes]
        own_mean[s], own_square[s] = moments(x.astype(F32))
        own_tail[s] = x[:, main:]
    done = 1
    for first, last in column_groups(columns):
        count = 3 * ((min(last, 3 * width) - first) // TRIPLE)
        for load in loads[done : done + count]:
            load.wait()
        done += count
        w = near_weights[:main, first:last]
        for s in range(sequences):
            own_acc[s, :, first:last] = dot(held[s // passes, s % passes, :, :main], w)
        near_sum[:, first:last] = dot(ones, w)
    far_weights[:TAIL] = near_weights[main:]
    loads[done].wait()
    high, low = split2(dot_nt(out_rows[...], w_head[...]))
    out_weights[:, :OUTW] = high
    out_weights[:, OUTW:] = low
    for load in loads[done + 1 :]:
        load.wait()


def cut(windows, features, *refs):
    outs, sem = refs[:-1], refs[-1]
    passes = features.shape[2]
    loads = [
        pltpu.make_async_copy(
            features.at[0, s // passes, s % passes, :, pl.ds(start, stop - start)],
            out,
            sem.at[i],
        )
        for i, ((s, start, stop), out) in enumerate(zip(windows, outs))
    ]
    for load in loads:
        load.start()
    for load in loads:
        load.wait()


def halves(x):
    odd = lax.axis_index("blk") % 2 == 1
    low, high, weights = x[:STRIDE], x[STRIDE:BLOCK], x[BLOCK:]
    own, other = jnp.where(odd, high, low), jnp.where(odd, low, high)
    if weights.shape[0]:
        own = jnp.concatenate([own, weights], axis=0)
        other = jnp.concatenate([other, weights], axis=0)
    return own, other


def sum_early(own, got, here, next_chip, second_chip):
    for t, out in enumerate((here, next_chip, second_chip)):
        out[...] = halves(own[t] + got[t])[0]


def sum_chip(own, got, *refs):
    here, next_chip, second_chip = refs[-3:]
    next_chip[...] = own[1] + got[1]
    second_chip[...] = own[2] + got[2]
    at = 0
    for i in range(0, len(refs) - 3, 3):
        a, b, c = refs[i : i + 3]
        here[at : at + a.shape[0]] = a[...] + b[...] + c[...]
        at += a.shape[0]
    here[at:] = halves(own[0] + got[0])[0]


def sum_far(here, across, first, second, mine, other):
    kept, passed = halves(first[...] + second[...])
    before = here.shape[0] - kept.shape[0]
    mine[:before] = here[:before] + across[:before]
    mine[before:] = here[before:] + across[before:] + kept
    other[...] = passed


def finish(mine, got, out):
    odd = lax.axis_index("blk") % 2 == 1
    packed = mine[STRIDE : STRIDE + PACKED]
    packed = jnp.where(odd, packed[:, LAT // 2 :], packed[:, : LAT // 2])
    plain = [packed[:, k * WINDOW : (k + 1) * WINDOW] for k in range(STRIDE // PACKED)]
    weights = dot(jnp.concatenate(plain, axis=0).astype(BF16), repeat_map())
    batch_count = out.shape[0]
    for b in range(batch_count):
        at = b * STRIDE + PACKED * (b > 0)
        total = mine[at : at + STRIDE]
        if b == batch_count - 1:
            total = total + got[...]
        out[b] = total / weights


def extend(
    s,
    arrived,
    own_acc,
    own_mean,
    own_square,
    own_tail,
    far_weights,
    token,
    acc,
    mean,
    square,
):
    del token
    x = arrived[...]
    near = own_mean[s], own_square[s]
    half = far_weights.shape[0] - TAIL
    mean[0], square[0] = merged(near, half, x.astype(F32))
    x = jnp.concatenate([own_tail[s], x], axis=1)
    for first, last in column_groups(own_acc.shape[2]):
        w = far_weights[: x.shape[1], first:last]
        acc[0, :, first:last] = own_acc[s, :, first:last] + dot(x, w)


def attend(
    s,
    near_count,
    width,
    offsets,
    arrived,
    own_acc,
    own_mean,
    own_square,
    own_tail,
    sums_in,
    far_weights,
    out_weights,
    *rest,
):
    first_pass = s % 2 == 0
    q_even, q_odd, keys, values, context = rest[-5:]
    rest = rest[:-5]
    if first_pass:
        _, guided_out = rest[:2]
        sums_out = rest[2:]
    else:
        spread_map, mask_tile, guided_in = rest[:3]
        mask_blocks = rest[3:-2]
        blocks, frame = rest[-2:]
    tokens, far_count = arrived.shape
    columns = own_acc.shape[2]
    half = far_weights.shape[0] - TAIL
    slab = s if own_acc.shape[0] > 1 else 0
    x = arrived[...]
    near = own_mean[slab], own_square[slab]
    mean, square = merged(near, near_count, x.astype(F32))
    scale = lax.rsqrt(square / (near_count + far_count) + 1e-05)
    offset = mean * scale
    if near_count == half:
        x = jnp.concatenate([own_tail[s], x], axis=1)
    rows = slice(TAIL + half - x.shape[1], TAIL + half)
    start = s == 0
    if start:
        x = jnp.concatenate([x, jnp.ones((16, x.shape[1]), BF16)], axis=0)
    factor = math.log2(math.e) / HEAD**0.5
    query_scale, query_offset = scale * factor, offset * factor
    first_head = iota((1, PAIR), 1) < HEAD
    none = jnp.zeros((tokens, PAIR), BF16)
    groups = column_groups(columns)
    direct = []

    def project(first, last):
        total = dot(x, far_weights[rows, first:last])
        sums = sums_in[0:8, first:last]
        if start:
            sums = sums + total[tokens : tokens + 8]
            sums_out[0][:, first:last] = sums
            total = total[:tokens]
        total = total + own_acc[slab, :, first:last]
        sums = sums[0:1]
        for p in range((min(last, 3 * width) - first) // TRIPLE):
            place = slice(first // 3 + p * PAIR, first // 3 + (p + 1) * PAIR)

            def part(j, by, less):
                places = slice(p * TRIPLE + j * PAIR, p * TRIPLE + (j + 1) * PAIR)
                return total[:, places] * by - less * sums[:, places]

            query = part(0, query_scale, query_offset).astype(BF16)
            q_even[:, place] = jnp.where(first_head, query, none)
            q_odd[:, place] = jnp.where(first_head, none, query)
            keys[:, place] = part(1, scale, offset).astype(BF16)
            values[:, place] = part(2, scale, offset).astype(BF16)
        if last > 3 * width:
            direct.append(total[:, 3 * width - first :])

    ones = jnp.ones((tokens, PAIR), BF16)
    ones_even = jnp.where(first_head, ones, none)
    ones_odd = jnp.where(first_head, none, ones)

    probs = {}

    def score(p):
        place = slice(p * PAIR, (p + 1) * PAIR)
        k = keys[:, place]
        both = []
        for q in (q_even, q_odd):
            scores = dot_nt(q[:, place], k)
            top = jnp.max(scores, axis=1, keepdims=True)
            both.append(jnp.exp2(scores - top).astype(BF16))
        probs[p] = jnp.concatenate(both, axis=1)

    def attention(p):
        place = slice(p * PAIR, (p + 1) * PAIR)
        v = values[:, place]
        stacked = jnp.concatenate(
            [
                jnp.concatenate([jnp.where(first_head, v, none), ones_even], axis=1),
                jnp.concatenate([jnp.where(first_head, none, v), ones_odd], axis=1),
            ],
            axis=0,
        )
        both = dot(probs.pop(p), stacked)
        context[:, place] = (both[:, :PAIR] / both[:, PAIR:]).astype(BF16)

    pairs = width // PAIR
    for g in groups:
        project(*g)
    score(0)
    for p in range(pairs):
        if p + 1 < pairs:
            score(p + 1)
        attention(p)
    out = dot(context[...], out_weights[...]) + direct[0]
    if first_pass:
        guided_out[...] = (1.0 - guidance) * out
        return
    guided = guidance * out + guided_in[...]
    tiled = dot(jnp.concatenate(split2(guided), axis=1), spread_map[...])
    lane_row = iota((1, PATCH * LAT), 1) % LAT // (LAT // GRID)
    spread = tiled[:GRID]
    for r in range(1, GRID):
        spread = jnp.where(lane_row == r, tiled[r * GRID : (r + 1) * GRID], spread)
    spread = spread * mask_tile[...]
    shift = window_shift(offsets)
    for h in range(HALVES):
        lanes = slice(h * LANES, (h + 1) * LANES)
        for a in range(PATCH):
            places = slice(a * LAT + h * LANES, a * LAT + (h + 1) * LANES)
            frame[pl.ds(a, GRID, stride=PATCH), :] = spread[:, places]
        rolled = to_frame(frame, shift)
        for t in range(BLOCKS):
            blocks[t, :BLOCK, lanes] = rolled[t * BLOCK : (t + 1) * BLOCK]
    for x in mask_blocks:
        blocks[:, BLOCK:] = x[...]


def call(kernel, args, outs, scratch=(), flops=0, limit=1 << 20, smem=0):
    specs, values = [], []
    for i, x in enumerate(args):
        space = pltpu.SMEM if i < smem else pltpu.VMEM
        if isinstance(x, tuple):
            x, space = x
            x = pltpu.with_memory_space_constraint(x, space)
        specs.append(pl.BlockSpec(memory_space=space))
        values.append(x)
    return pl.pallas_call(
        kernel,
        out_shape=[pltpu.VMEM(shape, dtype) for shape, dtype in outs],
        in_specs=specs,
        out_specs=[pl.BlockSpec(memory_space=pltpu.VMEM)] * len(outs),
        scratch_shapes=list(scratch),
        compiler_params=pltpu.CompilerParams(vmem_limit_bytes=limit),
        cost_estimate=pl.CostEstimate(flops=flops, bytes_accessed=1 << 20, transcendentals=0),
    )(*values)


def partner(x):
    count = lax.axis_size("blk")
    return lax.ppermute(x, "blk", [(i, i ^ 1) for i in range(count)])


def across(x):
    return lax.ppermute(x, "mp", [(0, 1), (1, 0)])


def moved(x, by):
    count, sides = lax.axis_size("blk"), lax.axis_size("mp")
    pairs = [
        (i * sides + m, (i + 2 * by) % count * sides + (m ^ (i % 2)))
        for i in range(count)
        for m in range(sides)
    ]
    return lax.ppermute(x, ("blk", "mp"), pairs)


def blend_early(blocks):
    part = (blocks.shape[1] - STRIDE, LAT)
    got = partner(blocks)
    here, first, second = call(sum_early, (blocks, got), [(part, F32)] * 3)
    count = lax.axis_size("blk")
    first = lax.ppermute(first, "blk", [(i, (i + 2) % count) for i in range(count)])
    second = lax.ppermute(second, "blk", [(i, (i + 4) % count) for i in range(count)])
    return here, first, second


def blend_last(blocks, early, batch_count):
    whole, part = blocks.shape[1:], (batch_count * STRIDE + PACKED, LAT)
    got = partner(blocks)
    here, first, second = call(
        sum_chip, (blocks, got, *early), [(part, F32), (whole, F32), (whole, F32)]
    )
    first = moved(first, 1)
    second = moved(second, 2)
    other_side = across(here)
    mine, other = call(
        sum_far, (here, other_side, first, second), [(part, F32), ((STRIDE, LAT), F32)]
    )
    return pl.pallas_call(
        finish,
        out_shape=jax.ShapeDtypeStruct((batch_count, STRIDE, LAT), F32),
        compiler_params=pltpu.CompilerParams(vmem_limit_bytes=1 << 20),
        name="finish",
    )(mine, partner(other))


def shards(features, w_query, w_key, w_value, w_out, w_head, offsets, blend_mask):
    batch_count, passes, tokens, half = features.shape[1:]
    width = w_query.shape[1]
    sequences = batch_count * passes
    columns = 3 * width + 2 * OUTW
    windows = [(s, 0, half) for s in range(sequences - 1)]
    split = max(half - LAST_COLUMNS, 0)
    if split:
        windows.append((sequences - 1, 0, split))
    windows.append((sequences - 1, split, half))
    arrived = []
    for group in (windows[:1], windows[1:]):
        parts = call(
            functools.partial(cut, group),
            ((features, pltpu.HBM),),
            [((tokens, stop - start), features.dtype) for _, start, stop in group],
            [pltpu.SemaphoreType.DMA((len(group),))],
        )
        for part in parts:
            arrived.append(across(part))
    outs = [
        ((sequences, tokens, columns), F32),
        ((sequences, tokens, 1), F32),
        ((sequences, tokens, 1), F32),
        ((sequences, tokens, TAIL), BF16),
        ((8, columns), F32),
        ((TAIL + half, columns), BF16),
        ((width, 2 * OUTW), BF16),
        ((4 * OUTW, PATCH * LAT), BF16),
        ((GRID, PATCH * LAT), F32),
        ((BLOCKS, PACKED, LAT), F32),
    ]
    weights = [(w, pltpu.HBM) for w in (w_query, w_key, w_value, w_out)]
    frame = [pltpu.VMEM((FRAME, LANES), F32)]
    prepared = call(
        prepare,
        (offsets, (features, pltpu.HBM), *weights, w_head.T, blend_mask),
        outs,
        frame
        + [
            pltpu.VMEM(features.shape[1:], features.dtype),
            pltpu.VMEM((half, columns), BF16),
            pltpu.VMEM(w_out.shape, BF16),
            pltpu.SemaphoreType.DMA((2 + 6 * (width // PAIR),)),
        ],
        2 * sequences * tokens * half * 3 * width,
        24 << 20,
        1,
    )
    acc, mean, square, tail, sums, far_weights, out_weights = prepared[:7]
    spread_map, mask_tile, mask_blocks = prepared[7:]
    own = (acc, mean, square)
    work = [pltpu.VMEM((tokens, width), BF16)] * 5
    flops = 2 * tokens * (half * 3 * width + 2 * tokens * width)
    early = []
    token = mask_blocks
    at = 0
    for s in range(sequences):
        near, near_count = own, half
        if arrived[at].shape[1] < half:
            near = tuple(
                call(
                    functools.partial(extend, s),
                    (arrived[at], *own, tail, far_weights, (token, pl.ANY)),
                    [((1, tokens, columns), F32), ((1, tokens, 1), F32), ((1, tokens, 1), F32)],
                    (),
                    2 * tokens * arrived[at].shape[1] * 3 * width,
                    8 << 20,
                )
            )
            near_count = half + arrived[at].shape[1]
            at += 1
        args = (offsets, arrived[at], *near, tail, sums, far_weights, out_weights)
        at += 1
        scratch = work
        if s % passes == 0:
            args += ((token, pl.ANY),)
            results = [((tokens, 2 * OUTW), F32)]
            if s == 0:
                results.append(((8, columns), F32))
        else:
            args += (spread_map, mask_tile, token)
            rows = BLOCK
            if s < passes:
                args += (mask_blocks,)
                rows += PACKED
            results = [((BLOCKS, rows, LAT), F32)]
            scratch = frame + work
        token, *more = call(
            functools.partial(attend, s, near_count, width),
            args,
            results,
            scratch,
            flops,
            16 << 20,
            1,
        )
        if more:
            (sums,) = more
        if s % passes:
            if s < sequences - 1:
                early += blend_early(token)
    return blend_last(token, early, batch_count)


def solution(mesh):
    return jax.shard_map(
        shards,
        mesh=mesh,
        in_specs=(
            P("blk", None, None, None, "mp"),
            P(None, "mp"),
            P(None, "mp"),
            P(None, "mp"),
            P("mp", None),
            P(),
            P("blk"),
            P("blk", None, None),
        ),
        out_specs=P(None, "blk", None),
        check_vma=False,
    )
```

```python
import functools
import math

import jax
import jax.numpy as jnp
from jax import lax
from jax.experimental import pallas as pl
from jax.experimental.pallas import tpu as pltpu
from jax.sharding import PartitionSpec as P


HEAD = 64
GRID = 16
PATCH = 4
CHAN = 4
STRIDE = 16
WINDOW = 64
OUTW = 64

guidance = 3.0


F32 = jnp.float32
BF16 = jnp.bfloat16
LAT = WINDOW * CHAN
LANES = 128
HALVES = LAT // LANES
BLOCK = 2 * STRIDE
BLOCKS = -(-(WINDOW + BLOCK - 1) // BLOCK)
FRAME = BLOCKS * BLOCK
PACKED = BLOCK * WINDOW // LAT
PAIR = 2 * HEAD
TRIPLE = 3 * PAIR
TAIL = 128
LAST_COLUMNS = 256


def dot(a, b):
    return jnp.dot(a, b, preferred_element_type=F32)


def dot_nt(a, b):
    return lax.dot_general(a, b, (((1,), (1,)), ((), ())), preferred_element_type=F32)


def moments(x):
    mean = jnp.mean(x, axis=1, keepdims=True)
    centred = x - mean
    return mean, jnp.sum(centred * centred, axis=1, keepdims=True)


def merged(near, near_count, x):
    mean, square = near
    count = near_count + x.shape[1]
    gap = x - mean
    total = jnp.sum(gap, axis=1, keepdims=True)
    square = square + jnp.sum(gap * gap, axis=1, keepdims=True)
    return mean + total * (1.0 / count), square - total * total * (1.0 / count)


def split2(x):
    high = x.astype(BF16)
    return high, (x - high.astype(F32)).astype(BF16)


def iota(shape, axis):
    return lax.broadcasted_iota(jnp.int32, shape, axis)


def repeat_map():
    return (iota((WINDOW, LAT), 1) // CHAN == iota((WINDOW, LAT), 0)).astype(BF16)


def column_groups(columns):
    pairs = columns // TRIPLE
    starts = [2 * TRIPLE * g for g in range(-(-pairs // 2))]
    return list(zip(starts, starts[1:] + [columns]))


def to_frame(frame, shift):
    frame[WINDOW:] = jnp.zeros((FRAME - WINDOW, LANES), F32)
    by = shift + STRIDE * (lax.axis_index("blk") % 2)
    return pltpu.roll(frame[...], by, 0)


def window_shift(offsets):
    return offsets[0] - STRIDE * lax.axis_index("blk")


def prepare(
    offsets,
    features,
    w_query,
    w_key,
    w_value,
    w_out,
    w_head,
    mask,
    own_acc,
    own_mean,
    own_square,
    own_tail,
    near_sum,
    far_weights,
    out_weights,
    mask_tile,
    mask_blocks,
    frame,
    held,
    near_weights,
    out_rows,
    sem,
):
    half = features.shape[-1]
    width = w_query.shape[1]
    sequences, _, columns = own_acc.shape
    passes = features.shape[2]
    pairs = width // PAIR
    side = lax.axis_index("mp")
    near = pl.ds(pl.multiple_of(side * half, LANES), half)
    far = pl.ds(pl.multiple_of((1 - side) * half, LANES), half)
    loads = [(features.at[0], held)]
    for p in range(pairs):
        for j, w in enumerate((w_query, w_key, w_value)):
            source = pl.ds(p * PAIR, PAIR)
            place = pl.ds(p * TRIPLE + j * PAIR, PAIR)
            loads.append((w.at[near, source], near_weights.at[:, place]))
    loads.append((w_out, out_rows))
    for p in range(pairs):
        for j, w in enumerate((w_query, w_key, w_value)):
            source = pl.ds(p * PAIR, PAIR)
            place = pl.ds(p * TRIPLE + j * PAIR, PAIR)
            loads.append((w.at[far, source], far_weights.at[pl.ds(TAIL, half), place]))
    loads = [pltpu.make_async_copy(a, b, sem.at[i]) for i, (a, b) in enumerate(loads)]
    for load in loads:
        load.start()
    shift = window_shift(offsets)
    plain = mask[0].astype(F32)
    wide = dot(plain.astype(BF16), repeat_map())
    for h in range(HALVES):
        lanes = slice(h * LANES, (h + 1) * LANES)
        frame[:WINDOW] = wide[:, lanes]
        for a in range(PATCH):
            places = slice(a * LAT + h * LANES, a * LAT + (h + 1) * LANES)
            mask_tile[:, places] = frame[pl.ds(a, GRID, stride=PATCH), :]
    frame[:WINDOW, :WINDOW] = 0.5 * plain
    frame[:WINDOW, WINDOW:] = jnp.zeros((WINDOW, LANES - WINDOW), F32)
    rolled = to_frame(frame, shift)
    for t in range(BLOCKS):
        for k in range(LAT // WINDOW):
            rows = slice(t * BLOCK + k * PACKED, t * BLOCK + (k + 1) * PACKED)
            mask_blocks[t, :, k * WINDOW : (k + 1) * WINDOW] = rolled[rows, :WINDOW]
    near_weights[:, 3 * width : 3 * width + OUTW] = w_head[:, near].T
    near_weights[:, 3 * width + OUTW :] = jnp.zeros((half, columns - 3 * width - OUTW), BF16)
    far_weights[TAIL:, 3 * width :] = jnp.zeros((half, columns - 3 * width), BF16)
    loads[0].wait()
    main = half - TAIL
    ones = jnp.ones((8, main), BF16)
    for s in range(sequences):
        x = held[s // passes, s % passes]
        own_mean[s], own_square[s] = moments(x.astype(F32))
        own_tail[s] = x[:, main:]
    done = 1
    for first, last in column_groups(columns):
        count = 3 * ((min(last, 3 * width) - first) // TRIPLE)
        for load in loads[done : done + count]:
            load.wait()
        done += count
        w = near_weights[:main, first:last]
        for s in range(sequences):
            own_acc[s, :, first:last] = dot(held[s // passes, s % passes, :, :main], w)
        near_sum[:, first:last] = dot(ones, w)
    far_weights[:TAIL] = near_weights[main:]
    loads[done].wait()
    high, low = split2(dot_nt(out_rows[...], w_head[...]))
    out_weights[:, :OUTW] = high
    out_weights[:, OUTW:] = low
    for load in loads[done + 1 :]:
        load.wait()


def cut(windows, features, *refs):
    outs, sem = refs[:-1], refs[-1]
    passes = features.shape[2]
    loads = [
        pltpu.make_async_copy(
            features.at[0, s // passes, s % passes, :, pl.ds(start, stop - start)],
            out,
            sem.at[i],
        )
        for i, ((s, start, stop), out) in enumerate(zip(windows, outs))
    ]
    for load in loads:
        load.start()
    for load in loads:
        load.wait()


def halves(x):
    odd = lax.axis_index("blk") % 2 == 1
    low, high, weights = x[:STRIDE], x[STRIDE:BLOCK], x[BLOCK:]
    own, other = jnp.where(odd, high, low), jnp.where(odd, low, high)
    if weights.shape[0]:
        own = jnp.concatenate([own, weights], axis=0)
        other = jnp.concatenate([other, weights], axis=0)
    return own, other


def sum_early(own, got, here, next_chip, second_chip):
    for t, out in enumerate((here, next_chip, second_chip)):
        out[...] = halves(own[t] + got[t])[0]


def sum_chip(own, got, *refs):
    here, next_chip, second_chip = refs[-3:]
    next_chip[...] = own[1] + got[1]
    second_chip[...] = own[2] + got[2]
    at = 0
    for i in range(0, len(refs) - 3, 3):
        a, b, c = refs[i : i + 3]
        here[at : at + a.shape[0]] = a[...] + b[...] + c[...]
        at += a.shape[0]
    here[at:] = halves(own[0] + got[0])[0]


def sum_far(here, across, first, second, mine, other):
    kept, passed = halves(first[...] + second[...])
    before = here.shape[0] - kept.shape[0]
    mine[:before] = here[:before] + across[:before]
    mine[before:] = here[before:] + across[before:] + kept
    other[...] = passed


def settle(mine, weights, *blended):
    odd = lax.axis_index("blk") % 2 == 1
    packed = mine[STRIDE : STRIDE + PACKED]
    packed = jnp.where(odd, packed[:, LAT // 2 :], packed[:, : LAT // 2])
    plain = [packed[:, k * WINDOW : (k + 1) * WINDOW] for k in range(STRIDE // PACKED)]
    weights[...] = dot(jnp.concatenate(plain, axis=0).astype(BF16), repeat_map())
    for b, out in enumerate(blended):
        at = b * STRIDE + PACKED * (b > 0)
        out[...] = mine[at : at + STRIDE] / weights[...]


def finish(mine, got, weights, *rest):
    blended, out = rest[:-1], rest[-1]
    for b, x in enumerate(blended):
        out[b] = x[...]
    out[len(blended)] = (mine[-STRIDE:] + got[...]) / weights[...]


def extend(
    s,
    arrived,
    own_acc,
    own_mean,
    own_square,
    own_tail,
    far_weights,
    token,
    acc,
    mean,
    square,
):
    del token
    x = arrived[...]
    near = own_mean[s], own_square[s]
    half = far_weights.shape[0] - TAIL
    mean[0], square[0] = merged(near, half, x.astype(F32))
    x = jnp.concatenate([own_tail[s], x], axis=1)
    for first, last in column_groups(own_acc.shape[2]):
        w = far_weights[: x.shape[1], first:last]
        acc[0, :, first:last] = own_acc[s, :, first:last] + dot(x, w)


def attend(
    s,
    near_count,
    width,
    offsets,
    arrived,
    own_acc,
    own_mean,
    own_square,
    own_tail,
    sums_in,
    far_weights,
    out_weights,
    *rest,
):
    first_pass = s % 2 == 0
    q_even, q_odd, keys, values, context = rest[-5:]
    rest = rest[:-5]
    if first_pass:
        _, guided_out = rest[:2]
        sums_out = rest[2:]
    else:
        mask_tile, guided_in = rest[:2]
        mask_blocks = rest[2:-2]
        blocks, frame = rest[-2:]
    tokens, far_count = arrived.shape
    columns = own_acc.shape[2]
    half = far_weights.shape[0] - TAIL
    slab = s if own_acc.shape[0] > 1 else 0
    x = arrived[...]
    near = own_mean[slab], own_square[slab]
    mean, square = merged(near, near_count, x.astype(F32))
    scale = lax.rsqrt(square / (near_count + far_count) + 1e-05)
    offset = mean * scale
    if near_count == half:
        x = jnp.concatenate([own_tail[s], x], axis=1)
    rows = slice(TAIL + half - x.shape[1], TAIL + half)
    start = s == 0
    if start:
        x = jnp.concatenate([x, jnp.ones((16, x.shape[1]), BF16)], axis=0)
    factor = math.log2(math.e) / HEAD**0.5
    query_scale, query_offset = scale * factor, offset * factor
    first_head = iota((1, PAIR), 1) < HEAD
    none = jnp.zeros((tokens, PAIR), BF16)
    groups = column_groups(columns)
    direct = []

    def project(first, last):
        total = dot(x, far_weights[rows, first:last])
        sums = sums_in[0:8, first:last]
        if start:
            sums = sums + total[tokens : tokens + 8]
            sums_out[0][:, first:last] = sums
            total = total[:tokens]
        total = total + own_acc[slab, :, first:last]
        sums = sums[0:1]
        for p in range((min(last, 3 * width) - first) // TRIPLE):
            place = slice(first // 3 + p * PAIR, first // 3 + (p + 1) * PAIR)

            def part(j, by, less):
                places = slice(p * TRIPLE + j * PAIR, p * TRIPLE + (j + 1) * PAIR)
                return total[:, places] * by - less * sums[:, places]

            query = part(0, query_scale, query_offset).astype(BF16)
            q_even[:, place] = jnp.where(first_head, query, none)
            q_odd[:, place] = jnp.where(first_head, none, query)
            keys[:, place] = part(1, scale, offset).astype(BF16)
            values[:, place] = part(2, scale, offset).astype(BF16)
        if last > 3 * width:
            direct.append(total[:, 3 * width - first :])

    ones = jnp.ones((tokens, PAIR), BF16)
    ones_even = jnp.where(first_head, ones, none)
    ones_odd = jnp.where(first_head, none, ones)

    probs = {}

    def score(p):
        place = slice(p * PAIR, (p + 1) * PAIR)
        k = keys[:, place]
        both = []
        for q in (q_even, q_odd):
            scores = dot_nt(q[:, place], k)
            top = jnp.max(scores, axis=1, keepdims=True)
            both.append(jnp.exp2(scores - top).astype(BF16))
        probs[p] = jnp.concatenate(both, axis=1)

    def attention(p):
        place = slice(p * PAIR, (p + 1) * PAIR)
        v = values[:, place]
        stacked = jnp.concatenate(
            [
                jnp.concatenate([jnp.where(first_head, v, none), ones_even], axis=1),
                jnp.concatenate([jnp.where(first_head, none, v), ones_odd], axis=1),
            ],
            axis=0,
        )
        both = dot(probs.pop(p), stacked)
        context[:, place] = (both[:, :PAIR] / both[:, PAIR:]).astype(BF16)

    pairs = width // PAIR
    for g in groups:
        project(*g)
    score(0)
    for p in range(pairs):
        if p + 1 < pairs:
            score(p + 1)
        attention(p)
    out = dot(context[...], out_weights[...]) + direct[0]
    if first_pass:
        guided_out[...] = (1.0 - guidance) * out
        return
    guided = guidance * out + guided_in[...]
    guided = guided + pltpu.roll(guided, OUTW, 1)
    part = OUTW // PATCH
    per_half = LANES // part
    group = iota((1, LANES), 1) // part
    spread = [[None] * HALVES for _ in range(PATCH)]
    for r in range(GRID):
        token_row = guided[r * GRID : (r + 1) * GRID]
        turned = [token_row]
        turned += [pltpu.roll(token_row, part * d, 1) for d in range(1, PATCH)]
        h, place = divmod(r, per_half)
        for a in range(PATCH):
            value = turned[(r - a) % PATCH]
            before = spread[a][h]
            spread[a][h] = value if before is None else jnp.where(group == place, value, before)
    shift = window_shift(offsets)
    for h in range(HALVES):
        lanes = slice(h * LANES, (h + 1) * LANES)
        for a in range(PATCH):
            places = slice(a * LAT + h * LANES, a * LAT + (h + 1) * LANES)
            frame[pl.ds(a, GRID, stride=PATCH), :] = spread[a][h] * mask_tile[:, places]
        rolled = to_frame(frame, shift)
        for t in range(BLOCKS):
            blocks[t, :BLOCK, lanes] = rolled[t * BLOCK : (t + 1) * BLOCK]
    for x in mask_blocks:
        blocks[:, BLOCK:] = x[...]


def call(kernel, args, outs, scratch=(), flops=0, limit=1 << 20, smem=0):
    specs, values = [], []
    for i, x in enumerate(args):
        space = pltpu.SMEM if i < smem else pltpu.VMEM
        if isinstance(x, tuple):
            x, space = x
            x = pltpu.with_memory_space_constraint(x, space)
        specs.append(pl.BlockSpec(memory_space=space))
        values.append(x)
    return pl.pallas_call(
        kernel,
        out_shape=[pltpu.VMEM(shape, dtype) for shape, dtype in outs],
        in_specs=specs,
        out_specs=[pl.BlockSpec(memory_space=pltpu.VMEM)] * len(outs),
        scratch_shapes=list(scratch),
        compiler_params=pltpu.CompilerParams(vmem_limit_bytes=limit),
        cost_estimate=pl.CostEstimate(flops=flops, bytes_accessed=1 << 20, transcendentals=0),
    )(*values)


def partner(x):
    count = lax.axis_size("blk")
    return lax.ppermute(x, "blk", [(i, i ^ 1) for i in range(count)])


def across(x):
    return lax.ppermute(x, "mp", [(0, 1), (1, 0)])


def moved(x, by):
    count, sides = lax.axis_size("blk"), lax.axis_size("mp")
    pairs = [
        (i * sides + m, (i + 2 * by) % count * sides + (m ^ (i % 2)))
        for i in range(count)
        for m in range(sides)
    ]
    return lax.ppermute(x, ("blk", "mp"), pairs)


def blend_early(blocks):
    part = (blocks.shape[1] - STRIDE, LAT)
    got = partner(blocks)
    here, first, second = call(sum_early, (blocks, got), [(part, F32)] * 3)
    count = lax.axis_size("blk")
    first = lax.ppermute(first, "blk", [(i, (i + 2) % count) for i in range(count)])
    second = lax.ppermute(second, "blk", [(i, (i + 4) % count) for i in range(count)])
    return here, first, second


def blend_last(blocks, early, batch_count):
    whole, part = blocks.shape[1:], (batch_count * STRIDE + PACKED, LAT)
    got = partner(blocks)
    here, first, second = call(
        sum_chip, (blocks, got, *early), [(part, F32), (whole, F32), (whole, F32)]
    )
    first = moved(first, 1)
    second = moved(second, 2)
    other_side = across(here)
    mine, other = call(
        sum_far, (here, other_side, first, second), [(part, F32), ((STRIDE, LAT), F32)]
    )
    got = partner(other)
    settled = call(settle, (mine,), [((STRIDE, LAT), F32)] * batch_count)
    return pl.pallas_call(
        finish,
        out_shape=jax.ShapeDtypeStruct((batch_count, STRIDE, LAT), F32),
        compiler_params=pltpu.CompilerParams(vmem_limit_bytes=1 << 20),
        name="finish",
    )(mine, got, *settled)


def shards(features, w_query, w_key, w_value, w_out, w_head, offsets, blend_mask):
    batch_count, passes, tokens, half = features.shape[1:]
    width = w_query.shape[1]
    sequences = batch_count * passes
    columns = 3 * width + 2 * OUTW
    windows = [(s, 0, half) for s in range(sequences - 1)]
    split = max(half - LAST_COLUMNS, 0)
    if split:
        windows.append((sequences - 1, 0, split))
    windows.append((sequences - 1, split, half))
    arrived = []
    for group in (windows[:1], windows[1:]):
        parts = call(
            functools.partial(cut, group),
            ((features, pltpu.HBM),),
            [((tokens, stop - start), features.dtype) for _, start, stop in group],
            [pltpu.SemaphoreType.DMA((len(group),))],
        )
        for part in parts:
            arrived.append(across(part))
    outs = [
        ((sequences, tokens, columns), F32),
        ((sequences, tokens, 1), F32),
        ((sequences, tokens, 1), F32),
        ((sequences, tokens, TAIL), BF16),
        ((8, columns), F32),
        ((TAIL + half, columns), BF16),
        ((width, 2 * OUTW), BF16),
        ((GRID, PATCH * LAT), F32),
        ((BLOCKS, PACKED, LAT), F32),
    ]
    weights = [(w, pltpu.HBM) for w in (w_query, w_key, w_value, w_out)]
    frame = [pltpu.VMEM((FRAME, LANES), F32)]
    prepared = call(
        prepare,
        (offsets, (features, pltpu.HBM), *weights, w_head.T, blend_mask),
        outs,
        frame
        + [
            pltpu.VMEM(features.shape[1:], features.dtype),
            pltpu.VMEM((half, columns), BF16),
            pltpu.VMEM(w_out.shape, BF16),
            pltpu.SemaphoreType.DMA((2 + 6 * (width // PAIR),)),
        ],
        2 * sequences * tokens * half * 3 * width,
        24 << 20,
        1,
    )
    acc, mean, square, tail, sums, far_weights, out_weights = prepared[:7]
    mask_tile, mask_blocks = prepared[7:]
    own = (acc, mean, square)
    work = [pltpu.VMEM((tokens, width), BF16)] * 5
    flops = 2 * tokens * (half * 3 * width + 2 * tokens * width)
    early = []
    token = mask_blocks
    at = 0
    for s in range(sequences):
        near, near_count = own, half
        if arrived[at].shape[1] < half:
            near = tuple(
                call(
                    functools.partial(extend, s),
                    (arrived[at], *own, tail, far_weights, (token, pl.ANY)),
                    [((1, tokens, columns), F32), ((1, tokens, 1), F32), ((1, tokens, 1), F32)],
                    (),
                    2 * tokens * arrived[at].shape[1] * 3 * width,
                    8 << 20,
                )
            )
            near_count = half + arrived[at].shape[1]
            at += 1
        args = (offsets, arrived[at], *near, tail, sums, far_weights, out_weights)
        at += 1
        scratch = work
        if s % passes == 0:
            args += ((token, pl.ANY),)
            results = [((tokens, 2 * OUTW), F32)]
            if s == 0:
                results.append(((8, columns), F32))
        else:
            args += (mask_tile, token)
            rows = BLOCK
            if s < passes:
                args += (mask_blocks,)
                rows += PACKED
            results = [((BLOCKS, rows, LAT), F32)]
            scratch = frame + work
        token, *more = call(
            functools.partial(attend, s, near_count, width),
            args,
            results,
            scratch,
            flops,
            16 << 20,
            1,
        )
        if more:
            (sums,) = more
        if s % passes:
            if s < sequences - 1:
                early += blend_early(token)
    return blend_last(token, early, batch_count)


def solution(mesh):
    return jax.shard_map(
        shards,
        mesh=mesh,
        in_specs=(
            P("blk", None, None, None, "mp"),
            P(None, "mp"),
            P(None, "mp"),
            P(None, "mp"),
            P("mp", None),
            P(),
            P("blk"),
            P("blk", None, None),
        ),
        out_specs=P(None, "blk", None),
        check_vma=False,
    )
```

```python
import functools
import math

import jax
import jax.numpy as jnp
from jax import lax
from jax.experimental import pallas as pl
from jax.experimental.pallas import tpu as pltpu
from jax.sharding import PartitionSpec as P


HEAD = 64
GRID = 16
PATCH = 4
CHAN = 4
STRIDE = 16
WINDOW = 64
OUTW = 64

guidance = 3.0


F32 = jnp.float32
BF16 = jnp.bfloat16
LAT = WINDOW * CHAN
LANES = 128
HALVES = LAT // LANES
BLOCK = 2 * STRIDE
BLOCKS = -(-(WINDOW + BLOCK - 1) // BLOCK)
FRAME = BLOCKS * BLOCK
PACKED = BLOCK * WINDOW // LAT
PAIR = 2 * HEAD
TRIPLE = 3 * PAIR
TAIL = 128
LAST_COLUMNS = 256


def dot(a, b):
    return jnp.dot(a, b, preferred_element_type=F32)


def dot_nt(a, b):
    return lax.dot_general(a, b, (((1,), (1,)), ((), ())), preferred_element_type=F32)


def moments(x):
    mean = jnp.mean(x, axis=1, keepdims=True)
    centred = x - mean
    return mean, jnp.sum(centred * centred, axis=1, keepdims=True)


def merged(near, near_count, x):
    mean, square = near
    count = near_count + x.shape[1]
    gap = x - mean
    total = jnp.sum(gap, axis=1, keepdims=True)
    square = square + jnp.sum(gap * gap, axis=1, keepdims=True)
    return mean + total * (1.0 / count), square - total * total * (1.0 / count)


def split2(x):
    high = x.astype(BF16)
    return high, (x - high.astype(F32)).astype(BF16)


def iota(shape, axis):
    return lax.broadcasted_iota(jnp.int32, shape, axis)


def repeat_map():
    return (iota((WINDOW, LAT), 1) // CHAN == iota((WINDOW, LAT), 0)).astype(BF16)


def column_groups(columns):
    pairs = columns // TRIPLE
    starts = [2 * TRIPLE * g for g in range(-(-pairs // 2))]
    return list(zip(starts, starts[1:] + [columns]))


def to_frame(frame, shift):
    frame[WINDOW:] = jnp.zeros((FRAME - WINDOW, LANES), F32)
    by = shift + STRIDE * (lax.axis_index("blk") % 2)
    return pltpu.roll(frame[...], by, 0)


def window_shift(offsets):
    return offsets[0] - STRIDE * lax.axis_index("blk")


def prepare(
    offsets,
    features,
    w_query,
    w_key,
    w_value,
    w_out,
    w_head,
    mask,
    own_acc,
    own_mean,
    own_square,
    own_tail,
    near_sum,
    far_weights,
    out_weights,
    mask_tile,
    mask_blocks,
    frame,
    held,
    near_weights,
    out_rows,
    sem,
):
    half = features.shape[-1]
    width = w_query.shape[1]
    sequences, _, columns = own_acc.shape
    passes = features.shape[2]
    pairs = width // PAIR
    side = lax.axis_index("mp")
    near = pl.ds(pl.multiple_of(side * half, LANES), half)
    far = pl.ds(pl.multiple_of((1 - side) * half, LANES), half)
    loads = [(features.at[0], held)]
    for p in range(pairs):
        for j, w in enumerate((w_query, w_key, w_value)):
            source = pl.ds(p * PAIR, PAIR)
            place = pl.ds(p * TRIPLE + j * PAIR, PAIR)
            loads.append((w.at[near, source], near_weights.at[:, place]))
    loads.append((w_out, out_rows))
    for p in range(pairs):
        for j, w in enumerate((w_query, w_key, w_value)):
            source = pl.ds(p * PAIR, PAIR)
            place = pl.ds(p * TRIPLE + j * PAIR, PAIR)
            loads.append((w.at[far, source], far_weights.at[pl.ds(TAIL, half), place]))
    loads = [pltpu.make_async_copy(a, b, sem.at[i]) for i, (a, b) in enumerate(loads)]
    for load in loads:
        load.start()
    shift = window_shift(offsets)
    plain = mask[0].astype(F32)
    wide = dot(plain.astype(BF16), repeat_map())
    for h in range(HALVES):
        lanes = slice(h * LANES, (h + 1) * LANES)
        frame[:WINDOW] = wide[:, lanes]
        for a in range(PATCH):
            places = slice(a * LAT + h * LANES, a * LAT + (h + 1) * LANES)
            mask_tile[:, places] = frame[pl.ds(a, GRID, stride=PATCH), :]
    frame[:WINDOW, :WINDOW] = 0.5 * plain
    frame[:WINDOW, WINDOW:] = jnp.zeros((WINDOW, LANES - WINDOW), F32)
    rolled = to_frame(frame, shift)
    for t in range(BLOCKS):
        for k in range(LAT // WINDOW):
            rows = slice(t * BLOCK + k * PACKED, t * BLOCK + (k + 1) * PACKED)
            mask_blocks[t, :, k * WINDOW : (k + 1) * WINDOW] = rolled[rows, :WINDOW]
    near_weights[:, 3 * width : 3 * width + OUTW] = w_head[:, near].T
    near_weights[:, 3 * width + OUTW :] = jnp.zeros((half, columns - 3 * width - OUTW), BF16)
    far_weights[TAIL:, 3 * width :] = jnp.zeros((half, columns - 3 * width), BF16)
    loads[0].wait()
    main = half - TAIL
    ones = jnp.ones((8, main), BF16)
    for s in range(sequences):
        x = held[s // passes, s % passes]
        own_mean[s], own_square[s] = moments(x.astype(F32))
        own_tail[s] = x[:, main:]
    done = 1
    for first, last in column_groups(columns):
        count = 3 * ((min(last, 3 * width) - first) // TRIPLE)
        for load in loads[done : done + count]:
            load.wait()
        done += count
        w = near_weights[:main, first:last]
        for s in range(sequences):
            own_acc[s, :, first:last] = dot(held[s // passes, s % passes, :, :main], w)
        near_sum[:, first:last] = dot(ones, w)
    far_weights[:TAIL] = near_weights[main:]
    loads[done].wait()
    high, low = split2(dot_nt(out_rows[...], w_head[...]))
    out_weights[:, :OUTW] = high
    out_weights[:, OUTW:] = low
    for load in loads[done + 1 :]:
        load.wait()


def cut(windows, with_moments, features, *refs):
    outs, sem = refs[: len(windows)], refs[-1]
    passes = features.shape[2]
    loads = [
        pltpu.make_async_copy(
            features.at[0, s // passes, s % passes, :, pl.ds(start, stop - start)],
            out,
            sem.at[i],
        )
        for i, ((s, start, stop), out) in enumerate(zip(windows, outs))
    ]
    for load in loads:
        load.start()
    for load in loads:
        load.wait()
    if with_moments:
        last = windows[-1][0]
        parts = [out[...].astype(F32) for (s, *_), out in zip(windows, outs) if s == last]
        both = jnp.concatenate(moments(jnp.concatenate(parts, axis=1)), axis=1)
        refs[-2][...] = jnp.concatenate([both] + [jnp.zeros_like(both)] * 3, axis=1).T


def halves(x):
    odd = lax.axis_index("blk") % 2 == 1
    low, high, weights = x[:STRIDE], x[STRIDE:BLOCK], x[BLOCK:]
    own, other = jnp.where(odd, high, low), jnp.where(odd, low, high)
    if weights.shape[0]:
        own = jnp.concatenate([own, weights], axis=0)
        other = jnp.concatenate([other, weights], axis=0)
    return own, other


def sum_early(own, got, here, next_chip, second_chip):
    for t, out in enumerate((here, next_chip, second_chip)):
        out[...] = halves(own[t] + got[t])[0]


def sum_chip(own, got, *refs):
    here, next_chip, second_chip = refs[-3:]
    next_chip[...] = own[1] + got[1]
    second_chip[...] = own[2] + got[2]
    at = 0
    for i in range(0, len(refs) - 3, 3):
        a, b, c = refs[i : i + 3]
        here[at : at + a.shape[0]] = a[...] + b[...] + c[...]
        at += a.shape[0]
    here[at:] = halves(own[0] + got[0])[0]


def sum_far(here, across, first, second, mine, other):
    kept, passed = halves(first[...] + second[...])
    before = here.shape[0] - kept.shape[0]
    mine[:before] = here[:before] + across[:before]
    mine[before:] = here[before:] + across[before:] + kept
    other[...] = passed


def settle(mine, weights, *blended):
    odd = lax.axis_index("blk") % 2 == 1
    packed = mine[STRIDE : STRIDE + PACKED]
    packed = jnp.where(odd, packed[:, LAT // 2 :], packed[:, : LAT // 2])
    plain = [packed[:, k * WINDOW : (k + 1) * WINDOW] for k in range(STRIDE // PACKED)]
    weights[...] = dot(jnp.concatenate(plain, axis=0).astype(BF16), repeat_map())
    for b, out in enumerate(blended):
        at = b * STRIDE + PACKED * (b > 0)
        out[...] = mine[at : at + STRIDE] / weights[...]


def finish(mine, got, weights, *rest):
    blended, out = rest[:-1], rest[-1]
    for b, x in enumerate(blended):
        out[b] = x[...]
    out[len(blended)] = (mine[-STRIDE:] + got[...]) / weights[...]


def query_factor():
    return math.log2(math.e) / HEAD**0.5


def extend(
    s,
    width,
    arrived,
    far_moments,
    own_acc,
    own_mean,
    own_square,
    own_tail,
    sums,
    far_weights,
    token,
    acc,
    scales,
):
    del token
    half = far_weights.shape[0] - TAIL
    moments_far = far_moments[...].T
    gap = moments_far[:, 0:1] - own_mean[s]
    mean = own_mean[s] + 0.5 * gap
    square = own_square[s] + moments_far[:, 1:2] + gap * gap * (0.5 * half)
    scale = lax.rsqrt(square / (2 * half) + 1e-05)
    scales[...] = scale
    offset = mean * scale
    factor = query_factor()
    x = jnp.concatenate([own_tail[s], arrived[...]], axis=1)
    for first, last in column_groups(own_acc.shape[2]):
        w = far_weights[: x.shape[1], first:last]
        total = own_acc[s, :, first:last] + dot(x, w)
        for at in range(first, last, PAIR):
            here = total[:, at - first : at - first + PAIR]
            if at < 3 * width:
                by = factor if at % TRIPLE == 0 else 1.0
                here = here * (scale * by) - (offset * by) * sums[0:1, at : at + PAIR]
            acc[:, at : at + PAIR] = here


def attend(
    s,
    width,
    offsets,
    arrived,
    own_acc,
    own_mean,
    own_square,
    own_tail,
    sums_in,
    far_weights,
    out_weights,
    *rest,
):
    first_pass = s % 2 == 0
    normalized = len(own_acc.shape) == 2
    q_even, q_odd, keys, values, context = rest[-5:]
    rest = rest[:-5]
    if first_pass:
        _, guided_out = rest[:2]
        sums_out = rest[2:]
    else:
        mask_tile, guided_in = rest[:2]
        mask_blocks = rest[2:-2]
        blocks, frame = rest[-2:]
    tokens, _ = arrived.shape
    columns = own_acc.shape[-1]
    half = far_weights.shape[0] - TAIL
    x = arrived[...]
    if normalized:
        scale = own_mean[...]
    else:
        near = own_mean[s], own_square[s]
        mean, square = merged(near, half, x.astype(F32))
        scale = lax.rsqrt(square / (2 * half) + 1e-05)
        offset = mean * scale
        x = jnp.concatenate([own_tail[s], x], axis=1)
    rows = slice(TAIL + half - x.shape[1], TAIL + half)
    start = s == 0
    if start:
        x = jnp.concatenate([x, jnp.ones((16, x.shape[1]), BF16)], axis=0)
    factor = query_factor()
    query_scale = scale * factor
    query_offset = None if normalized else offset * factor
    first_head = iota((1, PAIR), 1) < HEAD
    none = jnp.zeros((tokens, PAIR), BF16)
    groups = column_groups(columns)
    direct = []

    def project(first, last):
        total = dot(x, far_weights[rows, first:last])
        sums = None
        if normalized:
            before = own_acc[:, first:last]
        else:
            sums = sums_in[0:8, first:last]
            if start:
                sums = sums + total[tokens : tokens + 8]
                sums_out[0][:, first:last] = sums
                total = total[:tokens]
            total = total + own_acc[s, :, first:last]
            sums = sums[0:1]
        for p in range((min(last, 3 * width) - first) // TRIPLE):
            place = slice(first // 3 + p * PAIR, first // 3 + (p + 1) * PAIR)

            def part(j, by, less):
                places = slice(p * TRIPLE + j * PAIR, p * TRIPLE + (j + 1) * PAIR)
                if normalized:
                    return before[:, places] + total[:, places] * by
                return total[:, places] * by - less * sums[:, places]

            query = part(0, query_scale, query_offset).astype(BF16)
            q_even[:, place] = jnp.where(first_head, query, none)
            q_odd[:, place] = jnp.where(first_head, none, query)
            keys[:, place] = part(1, scale, None if normalized else offset).astype(BF16)
            values[:, place] = part(2, scale, None if normalized else offset).astype(BF16)
        if last > 3 * width:
            plain = before if normalized else total
            direct.append(plain[:, 3 * width - first :])

    ones = jnp.ones((tokens, PAIR), BF16)
    ones_even = jnp.where(first_head, ones, none)
    ones_odd = jnp.where(first_head, none, ones)

    probs = {}

    def score(p):
        place = slice(p * PAIR, (p + 1) * PAIR)
        k = keys[:, place]
        both = []
        for q in (q_even, q_odd):
            scores = dot_nt(q[:, place], k)
            top = jnp.max(scores, axis=1, keepdims=True)
            both.append(jnp.exp2(scores - top).astype(BF16))
        probs[p] = jnp.concatenate(both, axis=1)

    def attention(p):
        place = slice(p * PAIR, (p + 1) * PAIR)
        v = values[:, place]
        stacked = jnp.concatenate(
            [
                jnp.concatenate([jnp.where(first_head, v, none), ones_even], axis=1),
                jnp.concatenate([jnp.where(first_head, none, v), ones_odd], axis=1),
            ],
            axis=0,
        )
        both = dot(probs.pop(p), stacked)
        context[:, place] = (both[:, :PAIR] / both[:, PAIR:]).astype(BF16)

    pairs = width // PAIR
    for g in groups:
        project(*g)
    score(0)
    for p in range(pairs):
        if p + 1 < pairs:
            score(p + 1)
        attention(p)
    out = dot(context[...], out_weights[...]) + direct[0]
    if first_pass:
        guided_out[...] = (1.0 - guidance) * out
        return
    guided = guidance * out + guided_in[...]
    guided = guided + pltpu.roll(guided, OUTW, 1)
    part = OUTW // PATCH
    per_half = LANES // part
    group = iota((1, LANES), 1) // part
    spread = [[None] * HALVES for _ in range(PATCH)]
    for r in range(GRID):
        token_row = guided[r * GRID : (r + 1) * GRID]
        turned = [token_row]
        turned += [pltpu.roll(token_row, part * d, 1) for d in range(1, PATCH)]
        h, place = divmod(r, per_half)
        for a in range(PATCH):
            value = turned[(r - a) % PATCH]
            before = spread[a][h]
            spread[a][h] = value if before is None else jnp.where(group == place, value, before)
    shift = window_shift(offsets)
    for h in range(HALVES):
        lanes = slice(h * LANES, (h + 1) * LANES)
        for a in range(PATCH):
            places = slice(a * LAT + h * LANES, a * LAT + (h + 1) * LANES)
            frame[pl.ds(a, GRID, stride=PATCH), :] = spread[a][h] * mask_tile[:, places]
        rolled = to_frame(frame, shift)
        for t in range(BLOCKS):
            blocks[t, :BLOCK, lanes] = rolled[t * BLOCK : (t + 1) * BLOCK]
    for x in mask_blocks:
        blocks[:, BLOCK:] = x[...]


def call(kernel, args, outs, scratch=(), flops=0, limit=1 << 20, smem=0):
    specs, values = [], []
    for i, x in enumerate(args):
        space = pltpu.SMEM if i < smem else pltpu.VMEM
        if isinstance(x, tuple):
            x, space = x
            x = pltpu.with_memory_space_constraint(x, space)
        specs.append(pl.BlockSpec(memory_space=space))
        values.append(x)
    return pl.pallas_call(
        kernel,
        out_shape=[pltpu.VMEM(shape, dtype) for shape, dtype in outs],
        in_specs=specs,
        out_specs=[pl.BlockSpec(memory_space=pltpu.VMEM)] * len(outs),
        scratch_shapes=list(scratch),
        compiler_params=pltpu.CompilerParams(vmem_limit_bytes=limit),
        cost_estimate=pl.CostEstimate(flops=flops, bytes_accessed=1 << 20, transcendentals=0),
    )(*values)


def partner(x):
    count = lax.axis_size("blk")
    return lax.ppermute(x, "blk", [(i, i ^ 1) for i in range(count)])


def across(x):
    return lax.ppermute(x, "mp", [(0, 1), (1, 0)])


def moved(x, by):
    count, sides = lax.axis_size("blk"), lax.axis_size("mp")
    pairs = [
        (i * sides + m, (i + 2 * by) % count * sides + (m ^ (i % 2)))
        for i in range(count)
        for m in range(sides)
    ]
    return lax.ppermute(x, ("blk", "mp"), pairs)


def blend_early(blocks):
    part = (blocks.shape[1] - STRIDE, LAT)
    got = partner(blocks)
    here, first, second = call(sum_early, (blocks, got), [(part, F32)] * 3)
    count = lax.axis_size("blk")
    first = lax.ppermute(first, "blk", [(i, (i + 2) % count) for i in range(count)])
    second = lax.ppermute(second, "blk", [(i, (i + 4) % count) for i in range(count)])
    return here, first, second


def blend_last(blocks, early, batch_count):
    whole, part = blocks.shape[1:], (batch_count * STRIDE + PACKED, LAT)
    got = partner(blocks)
    here, first, second = call(
        sum_chip, (blocks, got, *early), [(part, F32), (whole, F32), (whole, F32)]
    )
    first = moved(first, 1)
    second = moved(second, 2)
    other_side = across(here)
    mine, other = call(
        sum_far, (here, other_side, first, second), [(part, F32), ((STRIDE, LAT), F32)]
    )
    got = partner(other)
    settled = call(settle, (mine,), [((STRIDE, LAT), F32)] * batch_count)
    return pl.pallas_call(
        finish,
        out_shape=jax.ShapeDtypeStruct((batch_count, STRIDE, LAT), F32),
        compiler_params=pltpu.CompilerParams(vmem_limit_bytes=1 << 20),
        name="finish",
    )(mine, got, *settled)


def shards(features, w_query, w_key, w_value, w_out, w_head, offsets, blend_mask):
    batch_count, passes, tokens, half = features.shape[1:]
    width = w_query.shape[1]
    sequences = batch_count * passes
    columns = 3 * width + 2 * OUTW
    windows = [(s, 0, half) for s in range(sequences - 1)]
    split = max(half - LAST_COLUMNS, 0)
    if split:
        windows.append((sequences - 1, 0, split))
    windows.append((sequences - 1, split, half))
    arrived = []
    for group in (windows[:1], windows[1:]):
        shapes = [((tokens, stop - start), features.dtype) for _, start, stop in group]
        with_moments = len(group) > 1
        if with_moments:
            shapes.append(((8, tokens), F32))
        parts = call(
            functools.partial(cut, group, with_moments),
            ((features, pltpu.HBM),),
            shapes,
            [pltpu.SemaphoreType.DMA((len(group),))],
            0,
            4 << 20,
        )
        if with_moments:
            far_moments = across(parts[-1])
        for part in parts[: len(group)]:
            arrived.append(across(part))
    outs = [
        ((sequences, tokens, columns), F32),
        ((sequences, tokens, 1), F32),
        ((sequences, tokens, 1), F32),
        ((sequences, tokens, TAIL), BF16),
        ((8, columns), F32),
        ((TAIL + half, columns), BF16),
        ((width, 2 * OUTW), BF16),
        ((GRID, PATCH * LAT), F32),
        ((BLOCKS, PACKED, LAT), F32),
    ]
    weights = [(w, pltpu.HBM) for w in (w_query, w_key, w_value, w_out)]
    frame = [pltpu.VMEM((FRAME, LANES), F32)]
    prepared = call(
        prepare,
        (offsets, (features, pltpu.HBM), *weights, w_head.T, blend_mask),
        outs,
        frame
        + [
            pltpu.VMEM(features.shape[1:], features.dtype),
            pltpu.VMEM((half, columns), BF16),
            pltpu.VMEM(w_out.shape, BF16),
            pltpu.SemaphoreType.DMA((2 + 6 * (width // PAIR),)),
        ],
        2 * sequences * tokens * half * 3 * width,
        24 << 20,
        1,
    )
    acc, mean, square, tail, sums, far_weights, out_weights = prepared[:7]
    mask_tile, mask_blocks = prepared[7:]
    own = (acc, mean, square)
    work = [pltpu.VMEM((tokens, width), BF16)] * 5
    flops = 2 * tokens * (half * 3 * width + 2 * tokens * width)
    early = []
    token = mask_blocks
    at = 0
    for s in range(sequences):
        near = own
        if arrived[at].shape[1] < half:
            normed, scales = call(
                functools.partial(extend, s, width),
                (arrived[at], far_moments, *own, tail, sums, far_weights, (token, pl.ANY)),
                [((tokens, columns), F32), ((tokens, 1), F32)],
                (),
                2 * tokens * arrived[at].shape[1] * 3 * width,
                8 << 20,
            )
            near = (normed, scales, scales)
            at += 1
        args = (offsets, arrived[at], *near, tail, sums, far_weights, out_weights)
        at += 1
        scratch = work
        if s % passes == 0:
            args += ((token, pl.ANY),)
            results = [((tokens, 2 * OUTW), F32)]
            if s == 0:
                results.append(((8, columns), F32))
        else:
            args += (mask_tile, token)
            rows = BLOCK
            if s < passes:
                args += (mask_blocks,)
                rows += PACKED
            results = [((BLOCKS, rows, LAT), F32)]
            scratch = frame + work
        token, *more = call(
            functools.partial(attend, s, width), args, results, scratch, flops, 16 << 20, 1
        )
        if more:
            (sums,) = more
        if s % passes:
            if s < sequences - 1:
                early += blend_early(token)
    return blend_last(token, early, batch_count)


def solution(mesh):
    return jax.shard_map(
        shards,
        mesh=mesh,
        in_specs=(
            P("blk", None, None, None, "mp"),
            P(None, "mp"),
            P(None, "mp"),
            P(None, "mp"),
            P("mp", None),
            P(),
            P("blk"),
            P("blk", None, None),
        ),
        out_specs=P(None, "blk", None),
        check_vma=False,
    )
```

```python
import functools
import math

import jax
import jax.numpy as jnp
from jax import lax
from jax.experimental import pallas as pl
from jax.experimental.pallas import tpu as pltpu
from jax.sharding import PartitionSpec as P


HEAD = 64
GRID = 16
PATCH = 4
CHAN = 4
STRIDE = 16
WINDOW = 64
OUTW = 64

guidance = 3.0


F32 = jnp.float32
BF16 = jnp.bfloat16
LAT = WINDOW * CHAN
LANES = 128
HALVES = LAT // LANES
BLOCK = 2 * STRIDE
BLOCKS = -(-(WINDOW + BLOCK - 1) // BLOCK)
FRAME = BLOCKS * BLOCK
PACKED = BLOCK * WINDOW // LAT
PAIR = 2 * HEAD
TRIPLE = 3 * PAIR
TAIL = 128
LAST_COLUMNS = 256


def dot(a, b):
    return jnp.dot(a, b, preferred_element_type=F32)


def dot_nt(a, b):
    return lax.dot_general(a, b, (((1,), (1,)), ((), ())), preferred_element_type=F32)


def moments(x):
    mean = jnp.mean(x, axis=1, keepdims=True)
    centred = x - mean
    return mean, jnp.sum(centred * centred, axis=1, keepdims=True)


def merged(near, near_count, x):
    mean, square = near
    count = near_count + x.shape[1]
    gap = x - mean
    total = jnp.sum(gap, axis=1, keepdims=True)
    square = square + jnp.sum(gap * gap, axis=1, keepdims=True)
    return mean + total * (1.0 / count), square - total * total * (1.0 / count)


def split2(x):
    high = x.astype(BF16)
    return high, (x - high.astype(F32)).astype(BF16)


def iota(shape, axis):
    return lax.broadcasted_iota(jnp.int32, shape, axis)


def repeat_map():
    return (iota((WINDOW, LAT), 1) // CHAN == iota((WINDOW, LAT), 0)).astype(BF16)


def column_groups(columns):
    pairs = columns // TRIPLE
    starts = [2 * TRIPLE * g for g in range(-(-pairs // 2))]
    return list(zip(starts, starts[1:] + [columns]))


def to_frame(frame, shift):
    frame[WINDOW:] = jnp.zeros((FRAME - WINDOW, LANES), F32)
    by = shift + STRIDE * (lax.axis_index("blk") % 2)
    return pltpu.roll(frame[...], by, 0)


def window_shift(offsets):
    return offsets[0] - STRIDE * lax.axis_index("blk")


def prepare(
    offsets,
    features,
    w_query,
    w_key,
    w_value,
    w_out,
    w_head,
    mask,
    own_acc,
    own_mean,
    own_square,
    own_tail,
    near_sum,
    far_weights,
    out_weights,
    mask_tile,
    mask_blocks,
    frame,
    held,
    near_weights,
    out_rows,
    sem,
):
    half = features.shape[-1]
    width = w_query.shape[1]
    sequences, _, columns = own_acc.shape
    passes = features.shape[2]
    pairs = width // PAIR
    side = lax.axis_index("mp")
    near = pl.ds(pl.multiple_of(side * half, LANES), half)
    far = pl.ds(pl.multiple_of((1 - side) * half, LANES), half)
    loads = [(features.at[0], held)]
    for p in range(pairs):
        for j, w in enumerate((w_query, w_key, w_value)):
            source = pl.ds(p * PAIR, PAIR)
            place = pl.ds(p * TRIPLE + j * PAIR, PAIR)
            loads.append((w.at[near, source], near_weights.at[:, place]))
    loads.append((w_out, out_rows))
    for p in range(pairs):
        for j, w in enumerate((w_query, w_key, w_value)):
            source = pl.ds(p * PAIR, PAIR)
            place = pl.ds(p * TRIPLE + j * PAIR, PAIR)
            loads.append((w.at[far, source], far_weights.at[pl.ds(TAIL, half), place]))
    loads = [pltpu.make_async_copy(a, b, sem.at[i]) for i, (a, b) in enumerate(loads)]
    for load in loads:
        load.start()
    shift = window_shift(offsets)
    plain = mask[0].astype(F32)
    wide = dot(plain.astype(BF16), repeat_map())
    for h in range(HALVES):
        lanes = slice(h * LANES, (h + 1) * LANES)
        frame[:WINDOW] = wide[:, lanes]
        for a in range(PATCH):
            places = slice(a * LAT + h * LANES, a * LAT + (h + 1) * LANES)
            mask_tile[:, places] = frame[pl.ds(a, GRID, stride=PATCH), :]
    frame[:WINDOW, :WINDOW] = 0.5 * plain
    frame[:WINDOW, WINDOW:] = jnp.zeros((WINDOW, LANES - WINDOW), F32)
    rolled = to_frame(frame, shift)
    for t in range(BLOCKS):
        for k in range(LAT // WINDOW):
            rows = slice(t * BLOCK + k * PACKED, t * BLOCK + (k + 1) * PACKED)
            mask_blocks[t, :, k * WINDOW : (k + 1) * WINDOW] = rolled[rows, :WINDOW]
    near_weights[:, 3 * width : 3 * width + OUTW] = w_head[:, near].T
    near_weights[:, 3 * width + OUTW :] = jnp.zeros((half, columns - 3 * width - OUTW), BF16)
    far_weights[TAIL:, 3 * width :] = jnp.zeros((half, columns - 3 * width), BF16)
    loads[0].wait()
    main = half - TAIL
    ones = jnp.ones((8, main), BF16)
    for s in range(sequences):
        x = held[s // passes, s % passes]
        own_mean[s], own_square[s] = moments(x.astype(F32))
        own_tail[s] = x[:, main:]
    done = 1
    for first, last in column_groups(columns):
        count = 3 * ((min(last, 3 * width) - first) // TRIPLE)
        for load in loads[done : done + count]:
            load.wait()
        done += count
        w = near_weights[:main, first:last]
        for s in range(sequences):
            own_acc[s, :, first:last] = dot(held[s // passes, s % passes, :, :main], w)
        near_sum[:, first:last] = dot(ones, w)
    far_weights[:TAIL] = near_weights[main:]
    loads[done].wait()
    high, low = split2(dot_nt(out_rows[...], w_head[...]))
    out_weights[:, :OUTW] = high
    out_weights[:, OUTW:] = low
    for load in loads[done + 1 :]:
        load.wait()


def cut(windows, with_moments, features, *refs):
    outs, sem = refs[: len(windows)], refs[-1]
    passes = features.shape[2]
    loads = [
        pltpu.make_async_copy(
            features.at[0, s // passes, s % passes, :, pl.ds(start, stop - start)],
            out,
            sem.at[i],
        )
        for i, ((s, start, stop), out) in enumerate(zip(windows, outs))
    ]
    for load in loads:
        load.start()
    for load in loads:
        load.wait()
    if with_moments:
        last = windows[-1][0]
        parts = [out[...].astype(F32) for (s, *_), out in zip(windows, outs) if s == last]
        both = jnp.concatenate(moments(jnp.concatenate(parts, axis=1)), axis=1)
        refs[-2][...] = jnp.concatenate([both] + [jnp.zeros_like(both)] * 3, axis=1).T


def halves(x):
    odd = lax.axis_index("blk") % 2 == 1
    low, high, weights = x[:STRIDE], x[STRIDE:BLOCK], x[BLOCK:]
    own, other = jnp.where(odd, high, low), jnp.where(odd, low, high)
    if weights.shape[0]:
        own = jnp.concatenate([own, weights], axis=0)
        other = jnp.concatenate([other, weights], axis=0)
    return own, other


def sum_early(own, got, here, next_chip, second_chip):
    for t, out in enumerate((here, next_chip, second_chip)):
        out[...] = halves(own[t] + got[t])[0]


def sum_chip(own, got, *refs):
    here, next_chip, second_chip = refs[-3:]
    next_chip[...] = own[1] + got[1]
    second_chip[...] = (own[2] + got[2]).astype(BF16)
    at = 0
    for i in range(0, len(refs) - 3, 3):
        a, b, c = refs[i : i + 3]
        here[at : at + a.shape[0]] = a[...] + b[...] + c[...]
        at += a.shape[0]
    here[at:] = halves(own[0] + got[0])[0]


def sum_far(here, across, first, second, mine, other):
    kept, passed = halves(first[...] + second[...].astype(F32))
    before = here.shape[0] - kept.shape[0]
    mine[:before] = here[:before] + across[:before]
    mine[before:] = here[before:] + across[before:] + kept
    other[...] = passed


def settle(mine, weights, *blended):
    odd = lax.axis_index("blk") % 2 == 1
    packed = mine[STRIDE : STRIDE + PACKED]
    packed = jnp.where(odd, packed[:, LAT // 2 :], packed[:, : LAT // 2])
    plain = [packed[:, k * WINDOW : (k + 1) * WINDOW] for k in range(STRIDE // PACKED)]
    weights[...] = dot(jnp.concatenate(plain, axis=0).astype(BF16), repeat_map())
    for b, out in enumerate(blended):
        at = b * STRIDE + PACKED * (b > 0)
        out[...] = mine[at : at + STRIDE] / weights[...]


def finish(mine, got, weights, *rest):
    blended, out = rest[:-1], rest[-1]
    for b, x in enumerate(blended):
        out[b] = x[...]
    out[len(blended)] = (mine[-STRIDE:] + got[...]) / weights[...]


def query_factor():
    return math.log2(math.e) / HEAD**0.5


def extend(
    s,
    width,
    arrived,
    far_moments,
    own_acc,
    own_mean,
    own_square,
    own_tail,
    sums,
    far_weights,
    token,
    acc,
    scales,
):
    del token
    half = far_weights.shape[0] - TAIL
    moments_far = far_moments[...].T
    gap = moments_far[:, 0:1] - own_mean[s]
    mean = own_mean[s] + 0.5 * gap
    square = own_square[s] + moments_far[:, 1:2] + gap * gap * (0.5 * half)
    scale = lax.rsqrt(square / (2 * half) + 1e-05)
    scales[...] = scale
    offset = mean * scale
    factor = query_factor()
    x = jnp.concatenate([own_tail[s], arrived[...]], axis=1)
    for first, last in column_groups(own_acc.shape[2]):
        w = far_weights[: x.shape[1], first:last]
        total = own_acc[s, :, first:last] + dot(x, w)
        for at in range(first, last, PAIR):
            here = total[:, at - first : at - first + PAIR]
            if at < 3 * width:
                by = factor if at % TRIPLE == 0 else 1.0
                here = here * (scale * by) - (offset * by) * sums[0:1, at : at + PAIR]
            acc[:, at : at + PAIR] = here


def attend(
    s,
    width,
    offsets,
    arrived,
    own_acc,
    own_mean,
    own_square,
    own_tail,
    sums_in,
    far_weights,
    out_weights,
    *rest,
):
    first_pass = s % 2 == 0
    normalized = len(own_acc.shape) == 2
    q_even, q_odd, keys, values, context = rest[-5:]
    rest = rest[:-5]
    if first_pass:
        _, guided_out = rest[:2]
        sums_out = rest[2:]
    else:
        mask_tile, guided_in = rest[:2]
        mask_blocks = rest[2:-2]
        blocks, frame = rest[-2:]
    tokens, _ = arrived.shape
    columns = own_acc.shape[-1]
    half = far_weights.shape[0] - TAIL
    x = arrived[...]
    if normalized:
        scale = own_mean[...]
    else:
        near = own_mean[s], own_square[s]
        mean, square = merged(near, half, x.astype(F32))
        scale = lax.rsqrt(square / (2 * half) + 1e-05)
        offset = mean * scale
        x = jnp.concatenate([own_tail[s], x], axis=1)
    rows = slice(TAIL + half - x.shape[1], TAIL + half)
    start = s == 0
    if start:
        x = jnp.concatenate([x, jnp.ones((16, x.shape[1]), BF16)], axis=0)
    factor = query_factor()
    query_scale = scale * factor
    query_offset = None if normalized else offset * factor
    first_head = iota((1, PAIR), 1) < HEAD
    none = jnp.zeros((tokens, PAIR), BF16)
    groups = column_groups(columns)
    direct = []

    def project(first, last):
        total = dot(x, far_weights[rows, first:last])
        sums = None
        if normalized:
            before = own_acc[:, first:last]
        else:
            sums = sums_in[0:8, first:last]
            if start:
                sums = sums + total[tokens : tokens + 8]
                sums_out[0][:, first:last] = sums
                total = total[:tokens]
            total = total + own_acc[s, :, first:last]
            sums = sums[0:1]
        for p in range((min(last, 3 * width) - first) // TRIPLE):
            place = slice(first // 3 + p * PAIR, first // 3 + (p + 1) * PAIR)

            def part(j, by, less):
                places = slice(p * TRIPLE + j * PAIR, p * TRIPLE + (j + 1) * PAIR)
                if normalized:
                    return before[:, places] + total[:, places] * by
                return total[:, places] * by - less * sums[:, places]

            query = part(0, query_scale, query_offset).astype(BF16)
            q_even[:, place] = jnp.where(first_head, query, none)
            q_odd[:, place] = jnp.where(first_head, none, query)
            keys[:, place] = part(1, scale, None if normalized else offset).astype(BF16)
            values[:, place] = part(2, scale, None if normalized else offset).astype(BF16)
        if last > 3 * width:
            plain = before if normalized else total
            direct.append(plain[:, 3 * width - first :])

    ones = jnp.ones((tokens, PAIR), BF16)
    ones_even = jnp.where(first_head, ones, none)
    ones_odd = jnp.where(first_head, none, ones)

    probs = {}

    def score(p):
        place = slice(p * PAIR, (p + 1) * PAIR)
        k = keys[:, place]
        both = []
        for q in (q_even, q_odd):
            scores = dot_nt(q[:, place], k)
            top = jnp.max(scores, axis=1, keepdims=True)
            both.append(jnp.exp2(scores - top).astype(BF16))
        probs[p] = jnp.concatenate(both, axis=1)

    def attention(p):
        place = slice(p * PAIR, (p + 1) * PAIR)
        v = values[:, place]
        stacked = jnp.concatenate(
            [
                jnp.concatenate([jnp.where(first_head, v, none), ones_even], axis=1),
                jnp.concatenate([jnp.where(first_head, none, v), ones_odd], axis=1),
            ],
            axis=0,
        )
        both = dot(probs.pop(p), stacked)
        context[:, place] = (both[:, :PAIR] / both[:, PAIR:]).astype(BF16)

    pairs = width // PAIR
    for g in groups:
        project(*g)
    score(0)
    for p in range(pairs):
        if p + 1 < pairs:
            score(p + 1)
        attention(p)
    out = dot(context[...], out_weights[...]) + direct[0]
    if first_pass:
        guided_out[...] = (1.0 - guidance) * out
        return
    guided = guidance * out + guided_in[...]
    guided = guided + pltpu.roll(guided, OUTW, 1)
    part = OUTW // PATCH
    per_half = LANES // part
    group = iota((1, LANES), 1) // part
    spread = [[None] * HALVES for _ in range(PATCH)]
    for r in range(GRID):
        token_row = guided[r * GRID : (r + 1) * GRID]
        turned = [token_row]
        turned += [pltpu.roll(token_row, part * d, 1) for d in range(1, PATCH)]
        h, place = divmod(r, per_half)
        for a in range(PATCH):
            value = turned[(r - a) % PATCH]
            before = spread[a][h]
            spread[a][h] = value if before is None else jnp.where(group == place, value, before)
    shift = window_shift(offsets)
    for h in range(HALVES):
        lanes = slice(h * LANES, (h + 1) * LANES)
        for a in range(PATCH):
            places = slice(a * LAT + h * LANES, a * LAT + (h + 1) * LANES)
            frame[pl.ds(a, GRID, stride=PATCH), :] = spread[a][h] * mask_tile[:, places]
        rolled = to_frame(frame, shift)
        for t in range(BLOCKS):
            blocks[t, :BLOCK, lanes] = rolled[t * BLOCK : (t + 1) * BLOCK]
    for x in mask_blocks:
        blocks[:, BLOCK:] = x[...]


def call(kernel, args, outs, scratch=(), flops=0, limit=1 << 20, smem=0):
    specs, values = [], []
    for i, x in enumerate(args):
        space = pltpu.SMEM if i < smem else pltpu.VMEM
        if isinstance(x, tuple):
            x, space = x
            x = pltpu.with_memory_space_constraint(x, space)
        specs.append(pl.BlockSpec(memory_space=space))
        values.append(x)
    return pl.pallas_call(
        kernel,
        out_shape=[pltpu.VMEM(shape, dtype) for shape, dtype in outs],
        in_specs=specs,
        out_specs=[pl.BlockSpec(memory_space=pltpu.VMEM)] * len(outs),
        scratch_shapes=list(scratch),
        compiler_params=pltpu.CompilerParams(vmem_limit_bytes=limit),
        cost_estimate=pl.CostEstimate(flops=flops, bytes_accessed=1 << 20, transcendentals=0),
    )(*values)


def partner(x):
    count = lax.axis_size("blk")
    return lax.ppermute(x, "blk", [(i, i ^ 1) for i in range(count)])


def across(x):
    return lax.ppermute(x, "mp", [(0, 1), (1, 0)])


def moved(x, by):
    count, sides = lax.axis_size("blk"), lax.axis_size("mp")
    pairs = [
        (i * sides + m, (i + 2 * by) % count * sides + (m ^ (i % 2)))
        for i in range(count)
        for m in range(sides)
    ]
    return lax.ppermute(x, ("blk", "mp"), pairs)


def blend_early(blocks):
    part = (blocks.shape[1] - STRIDE, LAT)
    got = partner(blocks)
    here, first, second = call(sum_early, (blocks, got), [(part, F32)] * 3)
    count = lax.axis_size("blk")
    first = lax.ppermute(first, "blk", [(i, (i + 2) % count) for i in range(count)])
    second = lax.ppermute(second, "blk", [(i, (i + 4) % count) for i in range(count)])
    return here, first, second


def blend_last(blocks, early, batch_count):
    whole, part = blocks.shape[1:], (batch_count * STRIDE + PACKED, LAT)
    got = partner(blocks)
    here, first, second = call(
        sum_chip, (blocks, got, *early), [(part, F32), (whole, F32), (whole, BF16)]
    )
    first = moved(first, 1)
    second = moved(second, 2)
    other_side = across(here)
    mine, other = call(
        sum_far, (here, other_side, first, second), [(part, F32), ((STRIDE, LAT), F32)]
    )
    got = partner(other)
    settled = call(settle, (mine,), [((STRIDE, LAT), F32)] * batch_count)
    return pl.pallas_call(
        finish,
        out_shape=jax.ShapeDtypeStruct((batch_count, STRIDE, LAT), F32),
        compiler_params=pltpu.CompilerParams(vmem_limit_bytes=1 << 20),
        name="finish",
    )(mine, got, *settled)


def shards(features, w_query, w_key, w_value, w_out, w_head, offsets, blend_mask):
    batch_count, passes, tokens, half = features.shape[1:]
    width = w_query.shape[1]
    sequences = batch_count * passes
    columns = 3 * width + 2 * OUTW
    windows = [(s, 0, half) for s in range(sequences - 1)]
    split = max(half - LAST_COLUMNS, 0)
    if split:
        windows.append((sequences - 1, 0, split))
    windows.append((sequences - 1, split, half))
    arrived = []
    for group in (windows[:1], windows[1:]):
        shapes = [((tokens, stop - start), features.dtype) for _, start, stop in group]
        with_moments = len(group) > 1
        if with_moments:
            shapes.append(((8, tokens), F32))
        parts = call(
            functools.partial(cut, group, with_moments),
            ((features, pltpu.HBM),),
            shapes,
            [pltpu.SemaphoreType.DMA((len(group),))],
            0,
            4 << 20,
        )
        if with_moments:
            far_moments = across(parts[-1])
        for part in parts[: len(group)]:
            arrived.append(across(part))
    outs = [
        ((sequences, tokens, columns), F32),
        ((sequences, tokens, 1), F32),
        ((sequences, tokens, 1), F32),
        ((sequences, tokens, TAIL), BF16),
        ((8, columns), F32),
        ((TAIL + half, columns), BF16),
        ((width, 2 * OUTW), BF16),
        ((GRID, PATCH * LAT), F32),
        ((BLOCKS, PACKED, LAT), F32),
    ]
    weights = [(w, pltpu.HBM) for w in (w_query, w_key, w_value, w_out)]
    frame = [pltpu.VMEM((FRAME, LANES), F32)]
    prepared = call(
        prepare,
        (offsets, (features, pltpu.HBM), *weights, w_head.T, blend_mask),
        outs,
        frame
        + [
            pltpu.VMEM(features.shape[1:], features.dtype),
            pltpu.VMEM((half, columns), BF16),
            pltpu.VMEM(w_out.shape, BF16),
            pltpu.SemaphoreType.DMA((2 + 6 * (width // PAIR),)),
        ],
        2 * sequences * tokens * half * 3 * width,
        24 << 20,
        1,
    )
    acc, mean, square, tail, sums, far_weights, out_weights = prepared[:7]
    mask_tile, mask_blocks = prepared[7:]
    own = (acc, mean, square)
    work = [pltpu.VMEM((tokens, width), BF16)] * 5
    flops = 2 * tokens * (half * 3 * width + 2 * tokens * width)
    early = []
    token = mask_blocks
    at = 0
    for s in range(sequences):
        near = own
        if arrived[at].shape[1] < half:
            normed, scales = call(
                functools.partial(extend, s, width),
                (arrived[at], far_moments, *own, tail, sums, far_weights, (token, pl.ANY)),
                [((tokens, columns), F32), ((tokens, 1), F32)],
                (),
                2 * tokens * arrived[at].shape[1] * 3 * width,
                8 << 20,
            )
            near = (normed, scales, scales)
            at += 1
        args = (offsets, arrived[at], *near, tail, sums, far_weights, out_weights)
        at += 1
        scratch = work
        if s % passes == 0:
            args += ((token, pl.ANY),)
            results = [((tokens, 2 * OUTW), F32)]
            if s == 0:
                results.append(((8, columns), F32))
        else:
            args += (mask_tile, token)
            rows = BLOCK
            if s < passes:
                args += (mask_blocks,)
                rows += PACKED
            results = [((BLOCKS, rows, LAT), F32)]
            scratch = frame + work
        token, *more = call(
            functools.partial(attend, s, width), args, results, scratch, flops, 16 << 20, 1
        )
        if more:
            (sums,) = more
        if s % passes:
            if s < sequences - 1:
                early += blend_early(token)
    return blend_last(token, early, batch_count)


def solution(mesh):
    return jax.shard_map(
        shards,
        mesh=mesh,
        in_specs=(
            P("blk", None, None, None, "mp"),
            P(None, "mp"),
            P(None, "mp"),
            P(None, "mp"),
            P("mp", None),
            P(),
            P("blk"),
            P("blk", None, None),
        ),
        out_specs=P(None, "blk", None),
        check_vma=False,
    )
```
